32 devices in a mesh: comp: 2 (over y), lat: 4 (over x, core), lon: 4 (over z).
Axes of the slice: x: 2, y: 2, z: 4, core: 2. Of those that a mesh axis runs over, the one named last changes fastest.
Arguments:
- state: float32 [2, 3, 32, 64, 512], P('comp', None, None, 'lat', 'lon'), may hold values from -6 to 6
- wave_push: float32 [2, 32], P('comp'), may hold values from 0.2 to 0.6
- wave_fill: float32 [2, 32], P('comp'), may hold values from 0.2 to 0.6
- vertical: float32 [2, 32, 32], P('comp'), may hold values from -0.5 to 1
- land_mask: int32 [64, 512], P('lat', 'lon'), may hold values 0 or 1
- tile_match: int32 [4, 4, 2], P('lat'), may hold values from 0 to 3, as said below
- cell_counts: int32 [4, 4, 2], P('lat'), may hold values from 16 to 2032, as said below
Outputs:
- advanced: float32 [2, 3, 32, 64, 512], P('comp', None, None, 'lat', 'lon')
The draws below stay inside these ranges and needn't reach their ends.
Inputs may be any that keep to these rules, and one draw needn't show every extreme that they name: tile_match(i, j, 0) = j, and tile_match(i, j, 1) is j - 1 or j + 1 taken modulo 4. cell_counts(i, j, 0) + cell_counts(i, j, 1) = 2048, with both entries positive multiples of 16.
All inputs are finite; a program needn't handle non-finite values. No bound on the sum of `land_mask` on one device may be relied on, other than what follows from the above.
Results may differ from the reference program's by a relative error of at most 0.0001.
Values sent between devices are 32-bit elements; how exact they have to be, the bound alone decides.
A program may use at most 64 MiB of HBM per device.

```python
import math
import jax
import jax.numpy as jnp
from jax import lax

LEVELS = 32
FIELDS = 3
CLAT = 16
CLON = 128
TILES_LAT = 4
TILES_LON = 4
NLAT = 64
NLON = 512


def draw_vertical(key, part):
    key_off, key_diag = jax.random.split(jax.random.fold_in(key, 5))
    spread = 0.08
    offdiag = jnp.clip(jax.random.normal(key_off, (2, LEVELS, LEVELS), jnp.float32) * spread, -0.5, 0.5)
    diagonal = 0.8 + 0.2 * jax.random.uniform(key_diag, (2, LEVELS), jnp.float32)
    identity = jnp.eye(LEVELS, dtype=jnp.float32)
    return offdiag * (1.0 - identity) + diagonal[:, :, None] * identity


def draw_tile_match(key, part):
    side = jax.random.randint(jax.random.fold_in(key, 11), (TILES_LAT, TILES_LON), 0, 2).astype(jnp.int32) * 2 - 1
    columns = jnp.arange(TILES_LON).astype(jnp.int32)[None, :]
    first = jnp.broadcast_to(columns, (TILES_LAT, TILES_LON))
    second = (columns + side) % TILES_LON
    return jnp.stack([first, second.astype(jnp.int32)], axis=2).astype(jnp.int32)


def draw_cell_counts(key, part):
    shifted = jax.random.randint(jax.random.fold_in(key, 13), (TILES_LAT, TILES_LON), 1, CLON).astype(jnp.int32)
    row_ids = jnp.arange(TILES_LAT).astype(jnp.int32)[:, None]
    col_ids = jnp.arange(TILES_LON).astype(jnp.int32)[None, :]
    shifted = jnp.where((row_ids == 0) & (col_ids == 0), jnp.ones_like(shifted), shifted).astype(jnp.int32)
    shifted = jnp.where((row_ids == 0) & (col_ids == 1), jnp.full_like(shifted, CLON - 1), shifted).astype(jnp.int32)
    return jnp.stack([CLAT * (CLON - shifted), CLAT * shifted], axis=2).astype(jnp.int32)


def plant(entries, stream_key, least, largest):
    place = [jax.random.randint(jax.random.fold_in(stream_key, axis), (), 0, length) for axis, length in enumerate(entries.shape)]
    main_axis = entries.shape.index(max(entries.shape))
    beside = place[:main_axis] + [(place[main_axis] + 1) % entries.shape[main_axis]] + place[main_axis + 1:]
    return entries.at[tuple(place)].set(least).at[tuple(beside)].set(largest)


def block_scale(key, shape, shards, low, largest):
    gain = 1.0
    for dim, blocks in shards:
        heights = jax.random.uniform(jax.random.fold_in(jax.random.fold_in(key, 6), dim), (blocks,), jnp.float32, low / len(shards), largest / len(shards))
        gain = gain * jnp.repeat(jnp.exp(heights), shape[dim] // blocks).reshape((-1,) + (1,) * (len(shape) - 1 - dim))
    return gain


def centred(own_key, extent, scale, limit, cuts=(), held_as=jnp.bfloat16):
    drawn = jax.random.normal(own_key, extent, jnp.float32) * scale
    if len(cuts) > 0:
        drawn = block_scale(own_key, extent, cuts, -0.22, 0.18) * drawn
    return jnp.clip(drawn, min=-limit, max=limit).astype(held_as)


def setup_inputs(seed: int = 0) -> dict:
    splits = jax.random.split(jax.random.key(seed), 8)
    return {
        "state": centred(splits[0], (2, FIELDS, LEVELS, NLAT, NLON), 1.0, 6.0, ((0, 2), (3, 4), (4, 4)), jnp.float32),
        "wave_push": jnp.clip(jnp.exp(math.log(0.6) - 1.0986123 * jax.random.uniform(splits[1], (2, LEVELS), jnp.float32) ** block_scale(splits[1], (2, LEVELS), ((0, 2),), -0.2, 0.2)), 0.2, 0.6),
        "wave_fill": jnp.clip(jnp.exp(math.log(0.6) - 1.0986123 * jax.random.uniform(splits[2], (2, LEVELS), jnp.float32) ** block_scale(splits[2], (2, LEVELS), ((0, 2),), -0.2, 0.2)), 0.2, 0.6),
        "vertical": draw_vertical(jax.random.fold_in(splits[7], 71), 0),
        "land_mask": plant((jax.random.randint(splits[4], (NLAT, NLON), 0, 10) < 7).astype(jnp.int32), jax.random.fold_in(splits[4], 1), 0, 1),
        "tile_match": draw_tile_match(jax.random.fold_in(splits[7], 71), 0),
        "cell_counts": draw_cell_counts(jax.random.fold_in(splits[7], 71), 0),
    }


KAPPA = 0.5
CORIOLIS = 0.4


def diff_x(field):
    return (jnp.roll(field, -1, 3) - jnp.roll(field, 1, 3)) * 0.5


def diff_y(field):
    padded = jnp.pad(field, ((0, 0), (0, 0), (1, 1), (0, 0)))
    return (padded[:, :, 2:] - padded[:, :, :-2]) * 0.5


def substep(fields, push, fill, vertical, mask, fcor):
    u_old, v_old, p_old = fields[:, 0], fields[:, 1], fields[:, 2]
    u_one = u_old - push * diff_x(p_old) + fcor * v_old
    v_one = v_old - push * diff_y(p_old) - fcor * u_old
    div = diff_x(u_one) + diff_y(v_one)
    p_one = p_old - fill * div
    p_two = jnp.einsum('cam,cmyx->cayx', vertical, p_one, precision=lax.Precision.HIGHEST)
    return jnp.stack([u_one * mask, v_one * mask, p_two * mask], axis=1)


def reference(state, wave_push, wave_fill, vertical, land_mask, tile_match, cell_counts):
    mask = jnp.stack([jnp.ones((NLAT, NLON), jnp.float32), land_mask.astype(jnp.float32)])[:, None]
    rows = jnp.arange(NLAT).astype(jnp.float32)
    fcor = (CORIOLIS * jnp.sin(math.pi * ((rows + 0.5) / NLAT - 0.5)))[None, None, :, None]
    push = wave_push[:, :, None, None]
    fill = wave_fill[:, :, None, None]
    surface = state[:, :, 0]
    fields = state
    for step in range(2):
        fields = substep(fields, push, fill, vertical, mask, fcor)
    tiles = surface.reshape(2, FIELDS, TILES_LAT, CLAT, TILES_LON, CLON).transpose(0, 1, 2, 4, 3, 5)
    ids = jnp.arange(TILES_LON).astype(jnp.int32)
    hits = (tile_match[:, :, :, None] == ids[None, None, None, :]).astype(jnp.float32)
    weight = jnp.sum(hits * cell_counts.astype(jnp.float32)[:, :, :, None], axis=2)
    to_ocean = jnp.einsum('ijt,fitpq->fijpq', weight, tiles[0], precision=lax.Precision.HIGHEST)
    to_ocean = to_ocean / jnp.sum(weight, axis=2)[None, :, :, None, None]
    to_atmos = jnp.einsum('ijt,fijpq->fitpq', weight, tiles[1], precision=lax.Precision.HIGHEST)
    to_atmos = to_atmos / jnp.sum(weight, axis=1)[None, :, :, None, None]
    remapped = jnp.stack([to_atmos, to_ocean]).transpose(0, 1, 2, 4, 3, 5).reshape(2, FIELDS, NLAT, NLON)
    flux = KAPPA * (remapped - surface) * mask
    top = fields[:, :, 0] + flux
    return jnp.concatenate([top[:, :, None], fields[:, :, 1:]], axis=2)
```

```python
import functools
import math

import jax
import jax.numpy as jnp
from jax import lax
from jax.experimental import pallas as pl
from jax.experimental.pallas import tpu as pltpu
from jax.sharding import PartitionSpec as P

KAPPA = 0.5
CORIOLIS = 0.4
MESH = pl.DeviceIdType.MESH
HALO = 4
SPAN = 8
SETS = 3
ORDER = (1, 0, 2)
SLOTS = (0, 1, 4, 5)
U, V, PR = 0, 1, 2


class Layout:
    def __init__(self, rows, cols):
        self.blocks = cols // SPAN
        self.half = self.blocks // 2
        own = range(HALO, rows + HALO)
        assert rows * SPAN == cols and rows + 2 * HALO <= SETS * self.half
        self.dense, self.shift, self.span = {}, {}, {}
        at = 0
        for r in ORDER:
            mine = [e for e in own if e % SETS == r]
            self.shift[r] = mine[0] // SETS - at
            self.span[r] = (mine[0] // SETS, mine[-1] // SETS)
            for e in mine:
                self.dense[e - HALO] = at
                at += 1
        self.beyond = ((HALO - 2, HALO - 1), (rows + HALO, rows + HALO + 1))
        self.north = self.beyond[1][0] // SETS - self.beyond[0][0] // SETS
        for k in (0, 1):
            low, high = self.beyond[0][k], self.beyond[1][k]
            assert low % SETS == high % SETS and low // SETS == k
            assert high // SETS == self.north + k
        taken = [
            (s + self.corner(side, ns)) % self.blocks
            for side in (0, 1)
            for ns in (0, 1)
            for s in SLOTS
        ]
        assert len(set(taken)) == len(taken)

    def corner(self, side, ns):
        return self.half * side + self.north * ns


def exchange(
    sizes,
    state,
    push_in,
    fill_in,
    vert_in,
    land_in,
    match_in,
    count_in,
    main,
    edge,
    flux,
    ext,
    mid,
    vone,
    vtwo,
    part,
    dense,
    push_v,
    fill_v,
    vert_v,
    land_v,
    match_v,
    count_v,
    own_s,
    land_y,
    side_out,
    side_in,
    corner_out,
    corner_in,
    surf,
    load_sem,
    send_sem,
    recv_sem,
):
    levels, rows, cols, n_lat, n_lon = sizes
    plan = Layout(rows, cols)
    groups = levels // 8
    comp = lax.axis_index("comp")
    lat = lax.axis_index("lat")
    lon = lax.axis_index("lon")
    west = lax.rem(lon + n_lon - 1, n_lon)
    east = lax.rem(lon + 1, n_lon)
    other = 1 - comp
    has = (lat > 0, lat < n_lat - 1)
    beside = (lat - 1, lat + 1)

    barrier = pltpu.get_barrier_semaphore()

    def greet(to):
        pl.semaphore_signal(barrier, inc=1, device_id=to, device_id_type=MESH)

    greet((comp, lat, west))
    greet((comp, lat, east))
    greet((other, lat, lon))
    for ns in (0, 1):

        @pl.when(has[ns])
        def _(ns=ns):
            for there in (west, east, lon):
                greet((comp, beside[ns], there))

    small = (
        (push_in, push_v),
        (fill_in, fill_v),
        (vert_in, vert_v),
        (land_in, land_v),
        (match_in, match_v),
        (count_in, count_v),
        (state.at[:, 0], own_s),
    )
    first = HALO
    last = HALO + rows - 1
    for f in (PR, U, V):
        for y in range(rows):
            pltpu.make_async_copy(
                state.at[f, :, y, :], ext.at[f, first + y], load_sem.at[f]
            ).start()
    loads = [
        pltpu.make_async_copy(src, dst, load_sem.at[3 + k])
        for k, (src, dst) in enumerate(small)
    ]
    for copy in loads:
        copy.start()

    def wait_field(f):
        own = ext.at[f, pl.ds(first, rows)]
        pltpu.make_async_copy(own, own, load_sem.at[f]).wait()

    for ns in (0, 1):

        @pl.when(jnp.logical_not(has[ns]))
        def _(ns=ns):
            start = 0 if ns == 0 else first + rows
            for f in (U, V, PR):
                ext[f, pl.ds(start, HALO)] = jnp.zeros((HALO, levels, cols), jnp.float32)
            land_y[ns] = jnp.zeros((8, cols), jnp.int32)
            for side in (0, 1):
                corner_in[side, ns] = jnp.zeros((8, cols), jnp.float32)

    @pl.when(has[0])
    def _():
        ext[U, 0] = jnp.zeros((levels, cols), jnp.float32)
        ext[V, 0] = jnp.zeros((levels, cols), jnp.float32)

    @pl.when(has[1])
    def _():
        ext[U, last + HALO] = jnp.zeros((levels, cols), jnp.float32)
        ext[V, last + HALO] = jnp.zeros((levels, cols), jnp.float32)

    present = [flag.astype(jnp.float32) for flag in has]
    lane = lax.broadcasted_iota(jnp.int32, (levels, cols), 1)
    lane8 = lax.broadcasted_iota(jnp.int32, (8, cols), 1)
    j, block = lax.rem(lane, SPAN), lane // SPAN
    j8, block8 = lax.rem(lane8, SPAN), lane8 // SPAN
    west8 = block8 < plan.half
    by_size = {levels: (j, block), 8: (j8, block8)}

    def is_own(size):
        jj, blk = by_size[size]
        return ((blk < plan.half) & (jj >= HALO)) | ((blk >= plan.half) & (jj < HALO))

    stack = lambda x: jnp.concatenate([x] * groups, axis=0)

    def coriolis(row):
        angle = (row.astype(jnp.float32) + 0.5) / (n_lat * rows) - 0.5
        return CORIOLIS * jnp.sin(math.pi * angle)

    base_row = lat * rows - HALO
    fcor = coriolis(
        lax.broadcasted_iota(jnp.int32, (rows + 2 * HALO, cols), 0) + base_row
    )
    local8 = lax.rem(block8, plan.half)
    strip_fcor = [stack(coriolis(SETS * local8 + r + base_row)) for r in range(SETS)]

    def roll(x, by):
        by = by % cols
        return pltpu.roll(x, by, 1) if by else x

    def pack(row):
        result = None
        for y in range(rows):
            d = plan.dense[y]
            turned = roll(row(y), SPAN * d + HALO)
            where = (block if turned.shape[0] == levels else block8) == d
            result = turned if result is None else jnp.where(where, turned, result)
        return result

    def pack_field(f):
        wait_field(f)
        packed = pack(lambda y: ext[f, first + y])
        dense[f] = packed
        return packed

    low = j < HALO
    qp = pack_field(PR)
    qu = pack_field(U)
    side_out[0, pl.ds(0, levels)] = jnp.where(low, qp, roll(qu, HALO))
    side_out[1, pl.ds(0, levels)] = jnp.where(low, roll(qu, -HALO), qp)
    qv = pack_field(V)
    mid_level = levels // 2
    half_low = low[:mid_level]
    v_low, v_high = qv[:mid_level], qv[mid_level:]
    side_out[0, pl.ds(levels, mid_level)] = jnp.where(half_low, v_low, roll(v_high, HALO))
    side_out[1, pl.ds(levels, mid_level)] = jnp.where(half_low, roll(v_high, -HALO), v_low)
    for copy in loads[:4]:
        copy.wait()
    dry = comp == 1
    mask = jnp.where(dry, land_v[...].astype(jnp.float32), 1.0)
    spread = jnp.broadcast_to
    qm = pack(lambda y: spread(mask[y : y + 1], (8, cols)))
    side_out[0, pl.ds(levels + mid_level, 8)] = qm
    side_out[1, pl.ds(levels + mid_level, 8)] = qm

    turn = {PR: 0, U: -2, V: 2}
    for ns in (0, 1):
        its = 1 - ns
        picked = (0, 1) if ns == 0 else (rows - 2, rows - 1)
        found = {}
        for f in (U, V, PR):
            total = jnp.zeros((8, cols), jnp.float32)
            for k, y in enumerate(picked):
                value = ext[f, first + y]
                for g in range(groups):
                    b = (SLOTS[g] + plan.corner(0, its) + 2 * k) % plan.blocks
                    piece = roll(value[8 * g : 8 * g + 8], SPAN * b + HALO + turn[f])
                    total = jnp.where(block8 == b, piece, total)
            found[f] = total
        to_east = jnp.where(j8 < 2, found[U], jnp.where(j8 < 4, found[PR], found[V]))
        to_west = jnp.where(j8 < 4, found[U], jnp.where(j8 < 6, found[PR], found[V]))
        corner_out[ns, 0] = to_east
        corner_out[ns, 1] = roll(to_west, SPAN * plan.half)

    def remote(src, dst, sent, got, to):
        return pltpu.make_async_remote_copy(
            src_ref=src,
            dst_ref=dst,
            send_sem=send_sem.at[sent],
            recv_sem=recv_sem.at[got],
            device_id=to,
            device_id_type=MESH,
        )

    def side_copy(k, to):
        return remote(side_out.at[k], side_in.at[k], k, k, (comp, lat, to))

    sides = [side_copy(0, east), side_copy(1, west)]

    def corner_copies(ns):
        return [
            remote(
                corner_out.at[ns, side],
                corner_in.at[side, 1 - ns],
                2 + 2 * ns + side,
                2 + 2 * (1 - ns) + side,
                (comp, beside[ns], (east, west)[side]),
            )
            for side in (0, 1)
        ]

    def row_copies(ns):
        its = 1 - ns
        base, peer = 6 + 3 * ns, 6 + 3 * its
        to = (comp, beside[ns], lon)
        if ns == 0:
            p_from, p_to, w_from, w_to = first, first + rows, first, first + rows
        else:
            p_from, p_to, w_from, w_to = last + 1 - HALO, 0, last + 2 - HALO, 1
        return [
            remote(
                ext.at[PR, pl.ds(p_from, HALO)],
                ext.at[PR, pl.ds(p_to, HALO)],
                base,
                peer,
                to,
            ),
            remote(
                ext.at[pl.ds(0, 2), pl.ds(w_from, HALO - 1)],
                ext.at[pl.ds(0, 2), pl.ds(w_to, HALO - 1)],
                base + 1,
                peer + 1,
                to,
            ),
            remote(
                land_in.at[pl.ds(0 if ns == 0 else rows - 8, 8)],
                land_y.at[its],
                base + 2,
                peer + 2,
                to,
            ),
        ]

    across = remote(state.at[:, 0], surf.at[0], 12, 12, (other, lat, lon))
    onward = [
        remote(surf.at[0], surf.at[k], 12 + k, 12 + k, (comp, lat, to))
        for k, to in ((1, east), (2, west))
    ]

    count_there = [flag.astype(jnp.int32) for flag in has]
    pl.semaphore_wait(barrier, 3 + 3 * (count_there[0] + count_there[1]))
    for copy in reversed(sides):
        copy.start()
    for ns in (0, 1):

        @pl.when(has[ns])
        def _(ns=ns):
            for copy in corner_copies(ns) + row_copies(ns):
                copy.start()

    across.start()

    diag = lax.broadcasted_iota(jnp.int32, (levels, levels), 0) == lax.broadcasted_iota(
        jnp.int32, (levels, levels), 1
    )

    def per_level(ref):
        wide = spread(ref[...], (levels, levels))
        column = jnp.sum(jnp.where(diag, wide, 0.0), axis=1, keepdims=True)
        return spread(column * 0.5, (levels, cols))

    hp = per_level(push_v)
    hf = per_level(fill_v)
    vert = vert_v[...]
    vert_hi = vert.astype(jnp.bfloat16).astype(jnp.float32)
    vert_cat = jnp.concatenate([vert_hi, vert_hi, vert - vert_hi], axis=1).astype(
        jnp.bfloat16
    )

    def split(x):
        hi = x.astype(jnp.bfloat16)
        lo = (x - hi.astype(jnp.float32)).astype(jnp.bfloat16)
        return jnp.concatenate([hi, lo, hi], axis=0)

    def product(pieces):
        result = jnp.dot(
            vert_cat,
            jnp.concatenate([split(x) for x in pieces], axis=1),
            preferred_element_type=jnp.float32,
        )
        return [result[:, i * cols : (i + 1) * cols] for i in range(len(pieces))]

    is_first, is_last = lane == 0, lane == cols - 1

    def span_x(x):
        return jnp.where(is_last, 0.0, roll(x, -1)) - jnp.where(is_first, 0.0, roll(x, 1))

    beyond_mask = []

    def keep(e):
        if e < first:
            return beyond_mask[0][e + 8 - first : e + 9 - first]
        if e > last:
            return beyond_mask[1][e - last - 1 : e - last]
        return mask[e - first : e - first + 1]

    def force(e):
        return fcor[e : e + 1]

    def advance_v(read, store, es):
        for e in es:
            v1 = read(V, e) - hp * (read(PR, e + 1) - read(PR, e - 1)) - force(e) * read(U, e)
            if e == first - 1:
                v1 = present[0] * v1
            if e == last + 1:
                v1 = present[1] * v1
            store[e] = v1

    def advance_u(read, e):
        u1 = read(U, e) + force(e) * read(V, e) - hp * span_x(read(PR, e))
        return u1, read(PR, e) - hf * span_x(u1)

    def add_v(store, e, value):
        return value - hf * (store[e + 1] - store[e - 1])

    def read_one(f, e):
        return ext[f, e]

    def read_two(f, e):
        return mid[f, e]

    def write_mid(f, e, value):
        mid[f, e] = keep(e) * value

    def write_main(f, e, value):
        main[f, e - first] = keep(e) * value

    def run(read, store, write, v_rows, u_rows, p_rows, v_kept, slot):
        advance_v(read, store, v_rows)
        for e in v_kept:
            write(V, e, store[e])
        ready = {}
        for e in u_rows:
            u1, partial = advance_u(read, e)
            write(U, e, u1)
            if e in p_rows:
                ready[e] = add_v(store, e, partial)
            else:
                part[slot[e]] = partial
        for e in p_rows:
            if e not in ready:
                ready[e] = add_v(store, e, part[slot[e]])
        for e, value in zip(p_rows, product([ready[e] for e in p_rows])):
            write(PR, e, value)

    slot_one = {first: 0, first + 1: 1, last - 1: 2, last: 3}
    slot_two = {first + 2: 4, first + 3: 5, last - 3: 6, last - 2: 7}
    span = lambda a, b: list(range(a, b + 1))
    run(
        read_one,
        vone,
        write_mid,
        span(first + 1, last - 1),
        span(first, last),
        span(first + 2, last - 2),
        span(first + 1, last - 1),
        slot_one,
    )
    run(
        read_two,
        vtwo,
        write_main,
        span(first + 3, last - 3),
        span(first + 2, last - 2),
        span(first + 4, last - 4),
        span(first + 3, last - 3),
        slot_two,
    )

    across.wait_recv()
    for copy in onward:
        copy.start()

    for ns in (0, 1):

        @pl.when(has[ns])
        def _(ns=ns):
            for copy in row_copies(1 - ns):
                copy.wait_recv()

    for ns in (0, 1):
        covered = jnp.where(dry, land_y[ns].astype(jnp.float32), 1.0)
        beyond_mask.append(present[ns] * covered)
    run(
        read_one,
        vone,
        write_mid,
        span(first - 3, first) + span(last, last + 3),
        [first - 2, first - 1, last + 1, last + 2],
        span(first - 2, first + 1) + span(last - 1, last + 2),
        [first - 1, first, last, last + 1],
        slot_one,
    )
    run(
        read_two,
        vtwo,
        write_main,
        span(first - 1, first + 2) + span(last - 2, last + 1),
        [first, first + 1, last - 1, last],
        span(first, first + 3) + span(last - 3, last),
        span(first, first + 2) + span(last - 2, last),
        slot_two,
    )

    own = is_own(levels)

    def place(lower, upper, rest, r, only_own):
        by = SPAN * plan.shift[r]
        jj, blk = by_size[lower.shape[0]]
        a, b = plan.span[r]
        in_west = (blk >= a) & (blk <= b)
        in_east = (blk >= plan.half + a) & (blk <= plan.half + b)
        if only_own:
            in_west, in_east = in_west & (jj >= HALO), in_east & (jj < HALO)
        return jnp.where(
            in_west,
            roll(lower, by),
            jnp.where(in_east, roll(upper, by + SPAN * plan.half), rest),
        )

    beyond_set = [plan.beyond[0][k] % SETS for k in (0, 1)]

    def place_beyond(below, above, k):
        b, t = k, plan.north + k
        size = below.shape[0]
        blk = by_size[size][1]
        both = jnp.where(blk == b, roll(below, SPAN * b + HALO), 0.0)
        both = jnp.where(blk == t, roll(above, SPAN * t + HALO), both)
        turned = roll(both, SPAN * plan.half)
        picked = jnp.where(blk < plan.half, both, turned)
        return jnp.where(is_own(size), picked, 0.0)

    zero = jnp.zeros((levels, cols), jnp.float32)
    zero8 = jnp.zeros((8, cols), jnp.float32)

    def beyond_rows(f):
        rest = [zero] * SETS
        for k in (0, 1):
            rest[beyond_set[k]] = place_beyond(
                ext[f, plan.beyond[0][k]], ext[f, plan.beyond[1][k]], k
            )
        return rest

    rest = [beyond_rows(f) for f in (U, V, PR)]
    rest_mask = [zero8] * SETS
    for k in (0, 1):
        rest_mask[beyond_set[k]] = place_beyond(
            spread(keep(plan.beyond[0][k]), (8, cols)),
            spread(keep(plan.beyond[1][k]), (8, cols)),
            k,
        )
    factor = [None] * SETS
    low_v, high_v = first - 1, last + 1
    for e, flag in ((low_v, present[0]), (high_v, present[1])):
        r = e % SETS
        at = local8 == e // SETS
        factor[r] = jnp.where(at, flag, 1.0 if factor[r] is None else factor[r])
    factor = [None if x is None else stack(x) for x in factor]

    def up(x):
        return [x[1], x[2], roll(x[0], -SPAN)]

    def down(x):
        return [roll(x[2], SPAN), x[0], x[1]]

    cut_low = (block >= plan.half) & (j == 0)
    cut_high = (block < plan.half) & (j == SPAN - 1)

    def strip_step(u, v, p, masks, only_own):
        def span_strip(x):
            ahead, back = roll(x, -1), roll(x, 1)
            change = jnp.where(cut_high, 0.0, ahead) - jnp.where(cut_low, 0.0, back)
            return jnp.where(own, change, 0.0) if only_own else change

        above, under = up(p), down(p)
        v1 = []
        for r in range(SETS):
            value = v[r] - hp * (above[r] - under[r]) - strip_fcor[r] * u[r]
            v1.append(value if factor[r] is None else factor[r] * value)
        u1 = [u[r] + strip_fcor[r] * v[r] - hp * span_strip(p[r]) for r in range(SETS)]
        above, under = up(v1), down(v1)
        p1 = [p[r] - hf * (span_strip(u1[r]) + above[r] - under[r]) for r in range(SETS)]
        p2 = product(p1)
        m = [stack(x) for x in masks]
        return (
            [m[r] * u1[r] for r in range(SETS)],
            [m[r] * v1[r] for r in range(SETS)],
            [m[r] * p2[r] for r in range(SETS)],
        )

    packed = [dense[f] for f in (U, V, PR)]
    strips = [
        [place(packed[f], packed[f], rest[f][r], r, True) for r in range(SETS)]
        for f in (U, V, PR)
    ]
    own_masks = [place(qm, qm, rest_mask[r], r, True) for r in range(SETS)]
    for _ in range(2):
        strips = strip_step(*strips, own_masks, True)
    for f in (U, V, PR):
        for r in range(SETS):
            edge[f, r] = strips[f][r]

    for k in (0, 1):
        sides[k].wait_recv()
    for ns in (0, 1):

        @pl.when(has[ns])
        def _(ns=ns):
            for copy in corner_copies(1 - ns):
                copy.wait_recv()

    got_w, got_e = (side_in[k, pl.ds(0, levels)] for k in (0, 1))
    vw, ve = (side_in[k, pl.ds(levels, mid_level)] for k in (0, 1))
    mw, me = (side_in[k, pl.ds(levels + mid_level, 8)] for k in (0, 1))
    lower = [None] * 3
    upper = [None] * 3
    packed = [dense[f] for f in (U, V, PR)]
    lower[PR] = jnp.where(low, got_w, packed[PR])
    upper[PR] = jnp.where(low, packed[PR], got_e)
    lower[U] = jnp.where(low, roll(got_w, -HALO), packed[U])
    upper[U] = jnp.where(low, packed[U], roll(got_e, HALO))
    lower[V] = jnp.where(
        low, jnp.concatenate([vw, roll(vw, -HALO)], axis=0), packed[V]
    )
    upper[V] = jnp.where(
        low, packed[V], jnp.concatenate([ve, roll(ve, HALO)], axis=0)
    )
    low8 = j8 < HALO
    corners = [[rest[f][r] for r in range(SETS)] for f in (U, V, PR)]
    for k in (0, 1):
        total = corner_in[0, 0]
        blocks = lambda side, ns: functools.reduce(
            jnp.logical_or,
            [
                block8 == (s + plan.corner(side, ns) + 2 * k) % plan.blocks
                for s in SLOTS[:groups]
            ],
        )
        for side, ns in ((0, 1), (1, 0), (1, 1)):
            total = jnp.where(blocks(side, ns), corner_in[side, ns], total)
        at = functools.reduce(
            jnp.logical_or,
            [
                (block == plan.corner(side, ns) + k) & (j // 2 == 1 + side)
                for side in (0, 1)
                for ns in (0, 1)
            ],
        )
        r = beyond_set[k]
        for f in (U, V, PR):
            turned = [roll(total, -SPAN * (SLOTS[g] + k) - turn[f]) for g in range(groups)]
            corners[f][r] = jnp.where(
                at, jnp.concatenate(turned, axis=0), corners[f][r]
            )
    strips = [
        [place(lower[f], upper[f], corners[f][r], r, False) for r in range(SETS)]
        for f in (U, V, PR)
    ]
    lower_mask, upper_mask = jnp.where(low8, mw, qm), jnp.where(low8, qm, me)
    masks = [place(lower_mask, upper_mask, rest_mask[r], r, False) for r in range(SETS)]
    for _ in range(2):
        strips = strip_step(*strips, masks, False)
    high = j >= HALO
    for f in (U, V, PR):
        for r in range(SETS):
            change = strips[f][r] - edge[f, r]
            edge[f, r] = jnp.where(high, change, roll(change, SPAN * plan.half))

    for copy in loads[4:]:
        copy.wait()
    count = count_v[...].astype(jnp.float32)
    match = match_v[...]
    tile = lax.broadcasted_iota(jnp.int32, match.shape, 1)

    def coef(peer):
        mine = jnp.where((tile == lon) & (match == peer), count, 0.0)
        theirs = jnp.where((tile == peer) & (match == lon), count, 0.0)
        chosen = jnp.where(dry, mine, theirs)
        total = jnp.sum(jnp.sum(chosen, axis=1, keepdims=True), axis=0, keepdims=True)
        return spread(total, (rows, cols))

    coefs = [coef(lon), coef(west), coef(east)]
    inverse = KAPPA * mask / (coefs[0] + coefs[1] + coefs[2])
    scaled = [c * inverse for c in coefs]
    for copy in onward:
        copy.wait_recv()
    for f in (U, V, PR):
        value = -KAPPA * mask * own_s[f]
        for k in range(3):
            value = value + scaled[k] * surf[k, f]
        flux[f] = value

    for copy in sides + [across] + onward:
        copy.wait_send()
    for ns in (0, 1):

        @pl.when(has[ns])
        def _(ns=ns):
            for copy in corner_copies(ns) + row_copies(ns):
                copy.wait_send()


def finish(sizes, main, edge, flux, out, held, sem):
    levels, rows, cols = sizes
    plan = Layout(rows, cols)
    lane = lax.broadcasted_iota(jnp.int32, (levels, cols), 1)
    near = (lane < HALO) | (lane >= cols - HALO)
    top = lax.broadcasted_iota(jnp.int32, (8, cols), 0) == 0
    for y in range(rows):
        e = y + HALO
        by = (-SPAN * (e // SETS) - HALO) % cols
        for f in (U, V, PR):
            change = pltpu.roll(edge[f, e % SETS], by, 1)
            value = main[f, y] + jnp.where(near, change, 0.0)
            added = jnp.broadcast_to(flux[f, y : y + 1], (8, cols))
            held[f, y, 0:8] = value[0:8] + jnp.where(top, added, 0.0)
            held[f, y, 8:levels] = value[8:]
            pltpu.make_async_copy(held.at[f, y], out.at[f, :, y, :], sem.at[f]).start()
    for f in (U, V, PR):
        pltpu.make_async_copy(held.at[f], held.at[f], sem.at[f]).wait()


def shards(n_lat, n_lon, state, push, fill, vertical, land, match, counts):
    _, fields, levels, rows, cols = state.shape
    assert fields == 3 and levels % 16 == 0 and levels <= 32 and rows >= 16 and n_lon > 2
    f32 = jnp.float32
    any_spec = pl.BlockSpec(memory_space=pl.ANY)
    vmem_spec = pl.BlockSpec(memory_space=pltpu.VMEM)
    tall = rows + 2 * HALO
    line = (levels, cols)
    side_rows = levels + levels // 2 + 8
    main, edge, flux = pl.pallas_call(
        functools.partial(exchange, (levels, rows, cols, n_lat, n_lon)),
        out_shape=[
            pltpu.VMEM((fields, rows) + line, f32),
            pltpu.VMEM((fields, SETS) + line, f32),
            pltpu.VMEM((fields, rows, cols), f32),
        ],
        in_specs=[any_spec] * 7,
        out_specs=[vmem_spec] * 3,
        scratch_shapes=[
            pltpu.VMEM((fields, tall) + line, f32),
            pltpu.VMEM((fields, tall) + line, f32),
            pltpu.VMEM((tall,) + line, f32),
            pltpu.VMEM((tall,) + line, f32),
            pltpu.VMEM((8,) + line, f32),
            pltpu.VMEM((fields,) + line, f32),
            pltpu.VMEM(push.shape, f32),
            pltpu.VMEM(fill.shape, f32),
            pltpu.VMEM(vertical.shape[1:], f32),
            pltpu.VMEM(land.shape, jnp.int32),
            pltpu.VMEM(match.shape[:0:-1], jnp.int32),
            pltpu.VMEM(counts.shape[:0:-1], jnp.int32),
            pltpu.VMEM((fields, rows, cols), f32),
            pltpu.VMEM((2, 8, cols), jnp.int32),
            pltpu.VMEM((2, side_rows, cols), f32),
            pltpu.VMEM((2, side_rows, cols), f32),
            pltpu.VMEM((2, 2, 8, cols), f32),
            pltpu.VMEM((2, 2, 8, cols), f32),
            pltpu.VMEM((3, fields, rows, cols), f32),
            pltpu.SemaphoreType.DMA((10,)),
            pltpu.SemaphoreType.DMA((15,)),
            pltpu.SemaphoreType.DMA((15,)),
        ],
        compiler_params=pltpu.CompilerParams(collective_id=0, has_side_effects=True),
        name="exchange",
    )(
        state[0],
        push,
        fill,
        vertical.reshape(vertical.shape[1:]),
        land,
        match[0].T,
        counts[0].T,
    )
    main, edge, flux = (
        pltpu.with_memory_space_constraint(x, pltpu.VMEM) for x in (main, edge, flux)
    )
    result = pl.pallas_call(
        functools.partial(finish, (levels, rows, cols)),
        out_shape=jax.ShapeDtypeStruct(state.shape[1:], f32),
        in_specs=[vmem_spec] * 3,
        out_specs=any_spec,
        scratch_shapes=[
            pltpu.VMEM((fields, rows) + line, f32),
            pltpu.SemaphoreType.DMA((3,)),
        ],
        name="finish",
    )(main, edge, flux)
    return result[None]


def solution(mesh):
    sizes = dict(mesh.shape)
    return jax.shard_map(
        functools.partial(shards, sizes["lat"], sizes["lon"]),
        mesh=mesh,
        in_specs=(
            P("comp", None, None, "lat", "lon"),
            P("comp", None),
            P("comp", None),
            P("comp", None, None),
            P("lat", "lon"),
            P("lat", None, None),
            P("lat", None, None),
        ),
        out_specs=P("comp", None, None, "lat", "lon"),
        check_vma=False,
    )
```

```python
import functools
import math

import jax
import jax.numpy as jnp
from jax import lax
from jax.experimental import pallas as pl
from jax.experimental.pallas import tpu as pltpu
from jax.sharding import PartitionSpec as P

KAPPA = 0.5
CORIOLIS = 0.4
MESH = pl.DeviceIdType.MESH
HALO = 4
SPAN = 8
SETS = 3
ORDER = (1, 0, 2)
SLOTS = (0, 1, 4, 5)
U, V, PR = 0, 1, 2
ROWS = 5


class Layout:
    def __init__(self, rows, cols):
        self.blocks = cols // SPAN
        self.half = self.blocks // 2
        own = range(HALO, rows + HALO)
        assert rows * SPAN == cols and rows + 2 * HALO <= SETS * self.half
        self.dense, self.shift, self.span = {}, {}, {}
        at = 0
        for r in ORDER:
            mine = [e for e in own if e % SETS == r]
            self.shift[r] = mine[0] // SETS - at
            self.span[r] = (mine[0] // SETS, mine[-1] // SETS)
            for e in mine:
                self.dense[e - HALO] = at
                at += 1
        self.beyond = ((HALO - 2, HALO - 1), (rows + HALO, rows + HALO + 1))
        self.north = self.beyond[1][0] // SETS - self.beyond[0][0] // SETS
        for k in (0, 1):
            low, high = self.beyond[0][k], self.beyond[1][k]
            assert low % SETS == high % SETS and low // SETS == k
            assert high // SETS == self.north + k
        taken = [
            (s + self.corner(side, ns)) % self.blocks
            for side in (0, 1)
            for ns in (0, 1)
            for s in SLOTS
        ]
        assert len(set(taken)) == len(taken)

    def corner(self, side, ns):
        return self.half * side + self.north * ns


def exchange(
    sizes,
    state,
    push_in,
    fill_in,
    vert_in,
    land_in,
    match_in,
    count_in,
    main,
    edge,
    flux,
    ext,
    mid,
    vone,
    vtwo,
    part,
    dense,
    push_v,
    fill_v,
    vert_v,
    land_v,
    match_v,
    count_v,
    land_y,
    side_out,
    side_in,
    row_out,
    row_in,
    corner_out,
    corner_in,
    surf,
    sizer,
    load_sem,
    send_sem,
    recv_sem,
    west_sem,
    other_sem,
):
    levels, rows, cols, n_lat, n_lon = sizes
    plan = Layout(rows, cols)
    groups = levels // 8
    comp = lax.axis_index("comp")
    lat = lax.axis_index("lat")
    lon = lax.axis_index("lon")
    west = lax.rem(lon + n_lon - 1, n_lon)
    east = lax.rem(lon + 1, n_lon)
    other = 1 - comp
    has = (lat > 0, lat < n_lat - 1)
    beside = (lat - 1, lat + 1)

    barrier = pltpu.get_barrier_semaphore()

    def greet(to):
        pl.semaphore_signal(barrier, inc=1, device_id=to, device_id_type=MESH)

    greet((comp, lat, west))
    for ns in (0, 1):

        @pl.when(has[ns])
        def _(ns=ns):
            greet((comp, beside[ns], lon))
            greet((comp, beside[ns], west))

    @pl.when(comp == 0)
    def _():
        for there in (lon, west, east):
            greet((other, lat, there))

    count = [flag.astype(jnp.int32) for flag in has]
    n_beside = count[0] + count[1]

    def enter(extra):
        pl.semaphore_wait(barrier, 1 + 2 * n_beside + extra)

        def tell(sem, to):
            pl.semaphore_signal(sem, inc=1, device_id=to, device_id_type=MESH)

        tell(west_sem, (comp, lat, east))
        for ns in (0, 1):

            @pl.when(has[ns])
            def _(ns=ns):
                tell(west_sem, (comp, beside[ns], east))

        if extra:
            for there in (lon, west, east):
                tell(other_sem, (other, lat, there))

    small = (
        (push_in, push_v),
        (fill_in, fill_v),
        (vert_in, vert_v),
        (land_in, land_v),
        (match_in, match_v),
        (count_in, count_v),
    )
    first = HALO
    last = HALO + rows - 1
    loads = [
        pltpu.make_async_copy(src, dst, load_sem.at[3 + k])
        for k, (src, dst) in enumerate(small)
    ]
    for copy in loads:
        copy.start()
    for f in (PR, U, V):
        for y in range(rows):
            pltpu.make_async_copy(
                state.at[f, :, y, :], ext.at[f, first + y], load_sem.at[f]
            ).start()

    def wait_field(f):
        own = ext.at[f, pl.ds(first, rows)]
        pltpu.make_async_copy(own, own, load_sem.at[f]).wait()

    for ns in (0, 1):

        @pl.when(jnp.logical_not(has[ns]))
        def _(ns=ns):
            row_in[ns] = jnp.zeros(row_in.shape[1:], jnp.float32)
            land_y[ns] = jnp.zeros((8, cols), jnp.int32)
            for side in (0, 1):
                corner_in[side, ns] = jnp.zeros((8, cols), jnp.float32)

    present = [flag.astype(jnp.float32) for flag in has]
    lane = lax.broadcasted_iota(jnp.int32, (levels, cols), 1)
    lane8 = lax.broadcasted_iota(jnp.int32, (8, cols), 1)
    j, block = lax.rem(lane, SPAN), lane // SPAN
    j8, block8 = lax.rem(lane8, SPAN), lane8 // SPAN
    west8 = block8 < plan.half
    by_size = {levels: (j, block), 8: (j8, block8)}

    def is_own(size):
        jj, blk = by_size[size]
        return ((blk < plan.half) & (jj >= HALO)) | ((blk >= plan.half) & (jj < HALO))

    stack = lambda x: jnp.concatenate([x] * groups, axis=0)

    def coriolis(row):
        angle = (row.astype(jnp.float32) + 0.5) / (n_lat * rows) - 0.5
        return CORIOLIS * jnp.sin(math.pi * angle)

    base_row = lat * rows - HALO
    fcor = coriolis(
        lax.broadcasted_iota(jnp.int32, (rows + 2 * HALO, cols), 0) + base_row
    )
    local8 = lax.rem(block8, plan.half)
    strip_fcor = [stack(coriolis(SETS * local8 + r + base_row)) for r in range(SETS)]

    def roll(x, by):
        by = by % cols
        return pltpu.roll(x, by, 1) if by else x

    def remote(src, dst, sent, got, to):
        return pltpu.make_async_remote_copy(
            src_ref=src,
            dst_ref=dst,
            send_sem=send_sem.at[sent],
            recv_sem=recv_sem.at[got],
            device_id=to,
            device_id_type=MESH,
        )

    def side_copy(k, to):
        return remote(side_out.at[k], side_in.at[k], 0, 0, (comp, lat, to))

    sides = [side_copy(0, east), side_copy(1, west)]

    def corner_copy(ns, side):
        return remote(
            corner_out.at[ns, side],
            corner_in.at[side, 1 - ns],
            1 + ns,
            1 + (1 - ns),
            (comp, beside[ns], (east, west)[side]),
        )

    def row_copies(ns):
        its = 1 - ns
        to = (comp, beside[ns], lon)
        start = 0 if ns == 0 else rows - 8
        return [
            remote(row_out.at[ns], row_in.at[its], 1 + ns, 3 + its, to),
            remote(land_in.at[pl.ds(start, 8)], land_y.at[its], 1 + ns, 3 + its, to),
        ]

    across = [
        remote(state.at[:, 0], surf.at[k], 0, 5, (other, lat, there))
        for k, there in enumerate((lon, east, west))
    ]

    side_size = side_out.shape[1]
    row_size = row_out.shape[1] + 8

    def wait_for(sem, size):
        view = sizer.at[pl.ds(0, size)]
        pltpu.make_async_copy(view, view, sem).wait()

    @pl.when(comp == 1)
    def _():
        enter(3)
        for copy in across:
            copy.start()

    def pack(row):
        result = None
        for y in range(rows):
            d = plan.dense[y]
            turned = roll(row(y), SPAN * d + HALO)
            where = (block if turned.shape[0] == levels else block8) == d
            result = turned if result is None else jnp.where(where, turned, result)
        return result

    def pack_field(f):
        packed = pack(lambda y: ext[f, first + y])
        dense[f] = packed
        return packed

    for copy in loads[:4]:
        copy.wait()
    dry = comp == 1
    mask = jnp.where(dry, land_v[...].astype(jnp.float32), 1.0)
    spread = jnp.broadcast_to
    diag = lax.broadcasted_iota(jnp.int32, (levels, levels), 0) == lax.broadcasted_iota(
        jnp.int32, (levels, levels), 1
    )

    def per_level(ref):
        wide = spread(ref[...], (levels, levels))
        column = jnp.sum(jnp.where(diag, wide, 0.0), axis=1, keepdims=True)
        return spread(column * 0.5, (levels, cols))

    hp = per_level(push_v)
    hf = per_level(fill_v)
    vert = vert_v[...]
    vert_hi = vert.astype(jnp.bfloat16).astype(jnp.float32)
    vert_cat = jnp.concatenate([vert_hi, vert_hi, vert - vert_hi], axis=1).astype(
        jnp.bfloat16
    )

    def split(x):
        hi = x.astype(jnp.bfloat16)
        lo = (x - hi.astype(jnp.float32)).astype(jnp.bfloat16)
        return jnp.concatenate([hi, lo, hi], axis=0)

    def product(pieces):
        result = jnp.dot(
            vert_cat,
            jnp.concatenate([split(x) for x in pieces], axis=1),
            preferred_element_type=jnp.float32,
        )
        return [result[:, i * cols : (i + 1) * cols] for i in range(len(pieces))]

    low = j < HALO
    wait_field(PR)
    qp = pack_field(PR)
    wait_field(U)
    qu = pack_field(U)
    side_out[0, pl.ds(0, levels)] = jnp.where(low, qp, roll(qu, HALO))
    side_out[1, pl.ds(0, levels)] = jnp.where(low, roll(qu, -HALO), qp)
    wait_field(V)
    turn = {PR: 0, U: -2, V: 2}
    for ns in (0, 1):
        its = 1 - ns
        picked = (0, 1) if ns == 0 else (rows - 2, rows - 1)
        found = {}
        for f in (U, V, PR):
            total = jnp.zeros((8, cols), jnp.float32)
            for k, y in enumerate(picked):
                value = ext[f, first + y]
                for g in range(groups):
                    b = (SLOTS[g] + plan.corner(0, its) + 2 * k) % plan.blocks
                    piece = roll(value[8 * g : 8 * g + 8], SPAN * b + HALO + turn[f])
                    total = jnp.where(block8 == b, piece, total)
            found[f] = total
        for f in (U, V, PR):
            row_out[ns, pl.ds(ROWS * levels + 8 * f, 8)] = found[f]
        to_east = jnp.where(j8 < 2, found[U], jnp.where(j8 < 4, found[PR], found[V]))
        to_west = jnp.where(j8 < 4, found[U], jnp.where(j8 < 6, found[PR], found[V]))
        corner_out[ns, 0] = to_east
        corner_out[ns, 1] = roll(to_west, SPAN * plan.half)

    @pl.when(comp == 0)
    def _():
        enter(0)

    for ns in (0, 1):

        @pl.when(has[ns])
        def _(ns=ns):
            corner_copy(ns, 0).start()

    qv = pack_field(V)
    mid_level = levels // 2
    half_low = low[:mid_level]
    v_low, v_high = qv[:mid_level], qv[mid_level:]
    side_out[0, pl.ds(levels, mid_level)] = jnp.where(half_low, v_low, roll(v_high, HALO))
    side_out[1, pl.ds(levels, mid_level)] = jnp.where(half_low, roll(v_high, -HALO), v_low)
    qm = pack(lambda y: spread(mask[y : y + 1], (8, cols)))
    side_out[0, pl.ds(levels + mid_level, 8)] = qm
    side_out[1, pl.ds(levels + mid_level, 8)] = qm

    sides[0].start()

    is_first, is_last = lane == 0, lane == cols - 1

    def span_x(x):
        return jnp.where(is_last, 0.0, roll(x, -1)) - jnp.where(is_first, 0.0, roll(x, 1))

    beyond_mask = []

    def keep(e):
        if e < first:
            return beyond_mask[0][e + 8 - first : e + 9 - first]
        if e > last:
            return beyond_mask[1][e - last - 1 : e - last]
        return mask[e - first : e - first + 1]

    def force(e):
        return fcor[e : e + 1]

    def advance_v(read, store, es):
        for e in es:
            v1 = read(V, e) - hp * (read(PR, e + 1) - read(PR, e - 1)) - force(e) * read(U, e)
            store[e] = v1

    def advance_u(read, e):
        u1 = read(U, e) + force(e) * read(V, e) - hp * span_x(read(PR, e))
        return u1, read(PR, e) - hf * span_x(u1)

    def add_v(store, e, value):
        return value - hf * (store[e + 1] - store[e - 1])

    def read_one(f, e):
        return ext[f, e]

    def read_two(f, e):
        return mid[f, e]

    def write_mid(f, e, value):
        mid[f, e] = keep(e) * value

    def write_main(f, e, value):
        main[f, e - first] = keep(e) * value

    def run(read, store, write, v_rows, u_rows, p_rows, v_kept, slot):
        advance_v(read, store, v_rows)
        for e in v_kept:
            write(V, e, store[e])
        ready = {}
        for e in u_rows:
            u1, partial = advance_u(read, e)
            write(U, e, u1)
            if e in p_rows:
                ready[e] = add_v(store, e, partial)
            else:
                part[slot[e]] = partial
        for e in p_rows:
            if e not in ready:
                ready[e] = add_v(store, e, part[slot[e]])
        for e, value in zip(p_rows, product([ready[e] for e in p_rows])):
            write(PR, e, value)

    slot_one = {first: 0, first + 1: 1, last - 1: 2, last: 3}
    slot_two = {first + 2: 4, first + 3: 5, last - 3: 6, last - 2: 7}
    span = lambda a, b: list(range(a, b + 1))

    toward = (1.0, -1.0)
    edges = ((first, first + 1, first + 2), (last, last - 1, last - 2))
    advance_v(read_one, vone, span(first + 1, first + 2) + span(last - 2, last - 1))
    for ns in (0, 1):
        a, b, c = edges[ns]
        sign = toward[ns]
        partial = {}
        for e in (a, b):
            u1, partial[e] = advance_u(read_one, e)
            mid[U, e] = keep(e) * u1
            part[slot_one[e]] = partial[e]
            if e == a:
                u_edge = u1
        w = ext[V, a] - sign * (hp * ext[PR, b]) - force(a) * ext[U, a]
        sent = (
            ext[PR, a],
            w,
            partial[a] - sign * (hf * vone[b]),
            partial[b] - sign * (hf * (vone[c] - w)),
            w - force(a) * u_edge,
        )
        for k, value in enumerate(sent):
            row_out[ns, pl.ds(k * levels, levels)] = value

    for even in (0, 1):
        for ns in (even, 1 - even):

            @pl.when(has[ns] & (lax.rem(lat, 2) == even))
            def _(ns=ns):
                for copy in row_copies(ns):
                    copy.start()

    run(
        read_one,
        vone,
        write_mid,
        span(first + 3, last - 3),
        span(first + 2, last - 2),
        span(first + 2, last - 2),
        span(first + 1, last - 1),
        slot_one,
    )
    run(
        read_two,
        vtwo,
        write_main,
        span(first + 3, last - 3),
        span(first + 2, last - 2),
        span(first + 4, last - 4),
        span(first + 3, last - 3),
        slot_two,
    )

    def send_west():
        pl.semaphore_wait(west_sem, 1 + n_beside)
        sides[1].start()
        for ns in (0, 1):

            @pl.when(has[ns])
            def _(ns=ns):
                corner_copy(ns, 1).start()

        @pl.when(comp == 0)
        def _():
            pl.semaphore_wait(other_sem, 3)
            for copy in across:
                copy.start()

    send_west()
    for ns in (0, 1):

        @pl.when(has[ns])
        def _(ns=ns):
            wait_for(recv_sem.at[3 + ns], row_size)

    for ns in (0, 1):
        covered = jnp.where(dry, land_y[ns].astype(jnp.float32), 1.0)
        beyond_mask.append(present[ns] * covered)
    def got(ns, k):
        return row_in[ns, pl.ds(k * levels, levels)]

    ready = {}
    for ns in (0, 1):
        r, r2, r3 = edges[ns]
        a, b = (r - 1, r - 2) if ns == 0 else (r + 1, r + 2)
        sign = -toward[ns]
        p_r = ext[PR, r]
        v_r = ext[V, r] - sign * (hp * (got(ns, 0) - ext[PR, r2])) - force(r) * ext[U, r]
        v_a = present[ns] * (got(ns, 1) + sign * (hp * p_r))
        vone[r] = v_r
        mid[V, r] = keep(r) * v_r
        ready[r] = part[slot_one[r]] - sign * (hf * (v_a - vone[r2]))
        ready[r2] = part[slot_one[r2]] - sign * (hf * (v_r - vone[r3]))
        ready[a] = got(ns, 2) + sign * (hf * v_r)
        ready[b] = got(ns, 3) + hf * (hp * p_r)
    for e, value in zip(ready, product(list(ready.values()))):
        mid[PR, e] = keep(e) * value
    for ns in (0, 1):
        r = edges[ns][0]
        a, b = (r - 1, r - 2) if ns == 0 else (r + 1, r + 2)
        sign = -toward[ns]
        own_part = keep(a) * (got(ns, 4) + sign * (hp * ext[PR, r]))
        vtwo[a] = present[ns] * (own_part - sign * (hp * (mid[PR, b] - mid[PR, r])))
    run(
        read_two,
        vtwo,
        write_main,
        span(first, first + 2) + span(last - 2, last),
        [first, first + 1, last - 1, last],
        span(first, first + 3) + span(last - 3, last),
        span(first, first + 2) + span(last - 2, last),
        slot_two,
    )

    own = is_own(levels)

    def place(lower, upper, rest, r, only_own):
        by = SPAN * plan.shift[r]
        jj, blk = by_size[lower.shape[0]]
        a, b = plan.span[r]
        in_west = (blk >= a) & (blk <= b)
        in_east = (blk >= plan.half + a) & (blk <= plan.half + b)
        if only_own:
            in_west, in_east = in_west & (jj >= HALO), in_east & (jj < HALO)
        return jnp.where(
            in_west,
            roll(lower, by),
            jnp.where(in_east, roll(upper, by + SPAN * plan.half), rest),
        )

    beyond_set = [plan.beyond[0][k] % SETS for k in (0, 1)]

    def place_beyond(below, above, k):
        b, t = k, plan.north + k
        size = below.shape[0]
        blk = by_size[size][1]
        both = jnp.where(blk == b, roll(below, SPAN * b + HALO), 0.0)
        both = jnp.where(blk == t, roll(above, SPAN * t + HALO), both)
        turned = roll(both, SPAN * plan.half)
        picked = jnp.where(blk < plan.half, both, turned)
        return jnp.where(is_own(size), picked, 0.0)

    zero = jnp.zeros((levels, cols), jnp.float32)
    zero8 = jnp.zeros((8, cols), jnp.float32)

    def slots_of(side, ns, k):
        return functools.reduce(
            jnp.logical_or,
            [
                block8 == (s + plan.corner(side, ns) + 2 * k) % plan.blocks
                for s in SLOTS[:groups]
            ],
        )

    def unfold(total, f, k):
        turned = [roll(total, -SPAN * (SLOTS[g] + k) - turn[f]) for g in range(groups)]
        return jnp.concatenate(turned, axis=0)

    def beyond_rows(f):
        rest = [zero] * SETS
        here = pl.ds(ROWS * levels + 8 * f, 8)
        for k in (0, 1):
            total = jnp.where(slots_of(0, 0, k), row_in[0, here], row_in[1, here])
            both = unfold(total, f, k)
            turned = roll(both, SPAN * plan.half)
            at = lax.rem(block, plan.half)
            picked = jnp.where(block < plan.half, both, turned)
            flag = ((at == k) | (at == plan.north + k)) & is_own(levels)
            rest[beyond_set[k]] = jnp.where(flag, picked, 0.0)
        return rest

    rest = [beyond_rows(f) for f in (U, V, PR)]
    rest_mask = [zero8] * SETS
    for k in (0, 1):
        rest_mask[beyond_set[k]] = place_beyond(
            spread(keep(plan.beyond[0][k]), (8, cols)),
            spread(keep(plan.beyond[1][k]), (8, cols)),
            k,
        )
    factor = [None] * SETS
    low_v, high_v = first - 1, last + 1
    for e, flag in ((low_v, present[0]), (high_v, present[1])):
        r = e % SETS
        at = local8 == e // SETS
        factor[r] = jnp.where(at, flag, 1.0 if factor[r] is None else factor[r])
    factor = [None if x is None else stack(x) for x in factor]

    def up(x):
        return [x[1], x[2], roll(x[0], -SPAN)]

    def down(x):
        return [roll(x[2], SPAN), x[0], x[1]]

    cut_low = (block >= plan.half) & (j == 0)
    cut_high = (block < plan.half) & (j == SPAN - 1)

    def strip_step(u, v, p, masks, only_own):
        def span_strip(x):
            ahead, back = roll(x, -1), roll(x, 1)
            change = jnp.where(cut_high, 0.0, ahead) - jnp.where(cut_low, 0.0, back)
            return jnp.where(own, change, 0.0) if only_own else change

        above, under = up(p), down(p)
        v1 = []
        for r in range(SETS):
            value = v[r] - hp * (above[r] - under[r]) - strip_fcor[r] * u[r]
            v1.append(value if factor[r] is None else factor[r] * value)
        u1 = [u[r] + strip_fcor[r] * v[r] - hp * span_strip(p[r]) for r in range(SETS)]
        above, under = up(v1), down(v1)
        p1 = [p[r] - hf * (span_strip(u1[r]) + above[r] - under[r]) for r in range(SETS)]
        p2 = product(p1)
        m = [stack(x) for x in masks]
        return (
            [m[r] * u1[r] for r in range(SETS)],
            [m[r] * v1[r] for r in range(SETS)],
            [m[r] * p2[r] for r in range(SETS)],
        )

    packed = [dense[f] for f in (U, V, PR)]
    strips = [
        [place(packed[f], packed[f], rest[f][r], r, True) for r in range(SETS)]
        for f in (U, V, PR)
    ]
    own_masks = [place(qm, qm, rest_mask[r], r, True) for r in range(SETS)]
    for _ in range(2):
        strips = strip_step(*strips, own_masks, True)
    for f in (U, V, PR):
        for r in range(SETS):
            edge[f, r] = strips[f][r]

    for copy in loads[4:]:
        copy.wait()
    tiles = count_v[...].astype(jnp.float32)
    match = match_v[...]
    tile = lax.broadcasted_iota(jnp.int32, match.shape, 1)

    def coef(peer):
        mine = jnp.where((tile == lon) & (match == peer), tiles, 0.0)
        theirs = jnp.where((tile == peer) & (match == lon), tiles, 0.0)
        chosen = jnp.where(dry, mine, theirs)
        total = jnp.sum(jnp.sum(chosen, axis=1, keepdims=True), axis=0, keepdims=True)
        return spread(total, (rows, cols))

    coefs = [coef(lon), coef(west), coef(east)]
    inverse = KAPPA * mask / (coefs[0] + coefs[1] + coefs[2])
    scaled = [c * inverse for c in coefs]
    for f in (U, V, PR):
        top = ext[f, pl.ds(first, rows), 0, :]
        flux[f] = -KAPPA * mask * top

    wait_for(recv_sem.at[0], 2 * side_size)
    for ns in (0, 1):

        @pl.when(has[ns])
        def _(ns=ns):
            wait_for(recv_sem.at[1 + ns], 16)

    got_w, got_e = (side_in[k, pl.ds(0, levels)] for k in (0, 1))
    vw, ve = (side_in[k, pl.ds(levels, mid_level)] for k in (0, 1))
    mw, me = (side_in[k, pl.ds(levels + mid_level, 8)] for k in (0, 1))
    lower = [None] * 3
    upper = [None] * 3
    packed = [dense[f] for f in (U, V, PR)]
    lower[PR] = jnp.where(low, got_w, packed[PR])
    upper[PR] = jnp.where(low, packed[PR], got_e)
    lower[U] = jnp.where(low, roll(got_w, -HALO), packed[U])
    upper[U] = jnp.where(low, packed[U], roll(got_e, HALO))
    lower[V] = jnp.where(
        low, jnp.concatenate([vw, roll(vw, -HALO)], axis=0), packed[V]
    )
    upper[V] = jnp.where(
        low, packed[V], jnp.concatenate([ve, roll(ve, HALO)], axis=0)
    )
    low8 = j8 < HALO
    corners = [[rest[f][r] for r in range(SETS)] for f in (U, V, PR)]
    for k in (0, 1):
        total = corner_in[0, 0]
        for side, ns in ((0, 1), (1, 0), (1, 1)):
            total = jnp.where(slots_of(side, ns, k), corner_in[side, ns], total)
        at = functools.reduce(
            jnp.logical_or,
            [
                (block == plan.corner(side, ns) + k) & (j // 2 == 1 + side)
                for side in (0, 1)
                for ns in (0, 1)
            ],
        )
        r = beyond_set[k]
        for f in (U, V, PR):
            corners[f][r] = jnp.where(at, unfold(total, f, k), corners[f][r])
    strips = [
        [place(lower[f], upper[f], corners[f][r], r, False) for r in range(SETS)]
        for f in (U, V, PR)
    ]
    lower_mask, upper_mask = jnp.where(low8, mw, qm), jnp.where(low8, qm, me)
    masks = [place(lower_mask, upper_mask, rest_mask[r], r, False) for r in range(SETS)]
    for _ in range(2):
        strips = strip_step(*strips, masks, False)
    high = j >= HALO
    for f in (U, V, PR):
        for r in range(SETS):
            change = strips[f][r] - edge[f, r]
            edge[f, r] = jnp.where(high, change, roll(change, SPAN * plan.half))

    wait_for(recv_sem.at[5], 9 * rows)
    for f in (U, V, PR):
        value = flux[f]
        for k in range(3):
            value = value + scaled[k] * surf[k, f]
        flux[f] = value

    wait_for(send_sem.at[0], 2 * side_size + 9 * rows)
    for ns in (0, 1):

        @pl.when(has[ns])
        def _(ns=ns):
            wait_for(send_sem.at[1 + ns], row_size + 16)


def finish(sizes, main, edge, flux, out, held, sem):
    levels, rows, cols = sizes
    plan = Layout(rows, cols)
    lane = lax.broadcasted_iota(jnp.int32, (levels, cols), 1)
    near = (lane < HALO) | (lane >= cols - HALO)
    top = lax.broadcasted_iota(jnp.int32, (8, cols), 0) == 0
    for y in range(rows):
        e = y + HALO
        by = (-SPAN * (e // SETS) - HALO) % cols
        for f in (U, V, PR):
            change = pltpu.roll(edge[f, e % SETS], by, 1)
            value = main[f, y] + jnp.where(near, change, 0.0)
            added = jnp.broadcast_to(flux[f, y : y + 1], (8, cols))
            held[f, y, 0:8] = value[0:8] + jnp.where(top, added, 0.0)
            held[f, y, 8:levels] = value[8:]
            pltpu.make_async_copy(held.at[f, y], out.at[f, :, y, :], sem.at[f]).start()
    for f in (U, V, PR):
        pltpu.make_async_copy(held.at[f], held.at[f], sem.at[f]).wait()


def shards(n_lat, n_lon, state, push, fill, vertical, land, match, counts):
    _, fields, levels, rows, cols = state.shape
    assert fields == 3 and levels % 16 == 0 and levels <= 32 and rows >= 16 and n_lon > 2
    f32 = jnp.float32
    any_spec = pl.BlockSpec(memory_space=pl.ANY)
    vmem_spec = pl.BlockSpec(memory_space=pltpu.VMEM)
    tall = rows + 2 * HALO
    line = (levels, cols)
    side_rows = levels + levels // 2 + 8
    main, edge, flux = pl.pallas_call(
        functools.partial(exchange, (levels, rows, cols, n_lat, n_lon)),
        out_shape=[
            pltpu.VMEM((fields, rows) + line, f32),
            pltpu.VMEM((fields, SETS) + line, f32),
            pltpu.VMEM((fields, rows, cols), f32),
        ],
        in_specs=[any_spec] * 7,
        out_specs=[vmem_spec] * 3,
        scratch_shapes=[
            pltpu.VMEM((fields, tall) + line, f32),
            pltpu.VMEM((fields, tall) + line, f32),
            pltpu.VMEM((tall,) + line, f32),
            pltpu.VMEM((tall,) + line, f32),
            pltpu.VMEM((8,) + line, f32),
            pltpu.VMEM((fields,) + line, f32),
            pltpu.VMEM(push.shape, f32),
            pltpu.VMEM(fill.shape, f32),
            pltpu.VMEM(vertical.shape[1:], f32),
            pltpu.VMEM(land.shape, jnp.int32),
            pltpu.VMEM(match.shape[:0:-1], jnp.int32),
            pltpu.VMEM(counts.shape[:0:-1], jnp.int32),
            pltpu.VMEM((2, 8, cols), jnp.int32),
            pltpu.VMEM((2, side_rows, cols), f32),
            pltpu.VMEM((2, side_rows, cols), f32),
            pltpu.VMEM((2, ROWS * levels + 24, cols), f32),
            pltpu.VMEM((2, ROWS * levels + 24, cols), f32),
            pltpu.VMEM((2, 2, 8, cols), f32),
            pltpu.VMEM((2, 2, 8, cols), f32),
            pltpu.VMEM((3, fields, rows, cols), f32),
            pltpu.VMEM((ROWS * levels + 48 + 9 * rows, cols), f32),
            pltpu.SemaphoreType.DMA((9,)),
            pltpu.SemaphoreType.DMA((3,)),
            pltpu.SemaphoreType.DMA((6,)),
            pltpu.SemaphoreType.REGULAR,
            pltpu.SemaphoreType.REGULAR,
        ],
        compiler_params=pltpu.CompilerParams(collective_id=0, has_side_effects=True),
        name="exchange",
    )(
        state[0],
        push,
        fill,
        vertical.reshape(vertical.shape[1:]),
        land,
        match[0].T,
        counts[0].T,
    )
    main, edge, flux = (
        pltpu.with_memory_space_constraint(x, pltpu.VMEM) for x in (main, edge, flux)
    )
    result = pl.pallas_call(
        functools.partial(finish, (levels, rows, cols)),
        out_shape=jax.ShapeDtypeStruct(state.shape[1:], f32),
        in_specs=[vmem_spec] * 3,
        out_specs=any_spec,
        scratch_shapes=[
            pltpu.VMEM((fields, rows) + line, f32),
            pltpu.SemaphoreType.DMA((3,)),
        ],
        name="finish",
    )(main, edge, flux)
    return result[None]


def solution(mesh):
    sizes = dict(mesh.shape)
    return jax.shard_map(
        functools.partial(shards, sizes["lat"], sizes["lon"]),
        mesh=mesh,
        in_specs=(
            P("comp", None, None, "lat", "lon"),
            P("comp", None),
            P("comp", None),
            P("comp", None, None),
            P("lat", "lon"),
            P("lat", None, None),
            P("lat", None, None),
        ),
        out_specs=P("comp", None, None, "lat", "lon"),
        check_vma=False,
    )
```

```python
import functools
import math

import jax
import jax.numpy as jnp
from jax import lax
from jax.experimental import pallas as pl
from jax.experimental.pallas import tpu as pltpu
from jax.sharding import PartitionSpec as P

KAPPA = 0.5
CORIOLIS = 0.4
MESH = pl.DeviceIdType.MESH
HALO = 4
SPAN = 8
SETS = 3
ORDER = (1, 0, 2)
SLOTS = (0, 1, 4, 5)
U, V, PR = 0, 1, 2
ROWS = 5


class Layout:
    def __init__(self, rows, cols):
        self.blocks = cols // SPAN
        self.half = self.blocks // 2
        own = range(HALO, rows + HALO)
        assert rows * SPAN == cols and rows + 2 * HALO <= SETS * self.half
        self.dense, self.shift, self.span = {}, {}, {}
        at = 0
        for r in ORDER:
            mine = [e for e in own if e % SETS == r]
            self.shift[r] = mine[0] // SETS - at
            self.span[r] = (mine[0] // SETS, mine[-1] // SETS)
            for e in mine:
                self.dense[e - HALO] = at
                at += 1
        self.beyond = ((HALO - 2, HALO - 1), (rows + HALO, rows + HALO + 1))
        self.north = self.beyond[1][0] // SETS - self.beyond[0][0] // SETS
        for k in (0, 1):
            low, high = self.beyond[0][k], self.beyond[1][k]
            assert low % SETS == high % SETS and low // SETS == k
            assert high // SETS == self.north + k
        taken = [
            (s + self.corner(side, ns)) % self.blocks
            for side in (0, 1)
            for ns in (0, 1)
            for s in SLOTS
        ]
        assert len(set(taken)) == len(taken)

    def corner(self, side, ns):
        return self.half * side + self.north * ns


def exchange(
    sizes,
    state,
    push_in,
    fill_in,
    vert_in,
    land_in,
    match_in,
    count_in,
    main,
    edge,
    flux,
    ext,
    mid,
    vone,
    vtwo,
    part,
    dense,
    push_v,
    fill_v,
    vert_v,
    land_v,
    match_v,
    count_v,
    land_y,
    side_out,
    side_in,
    row_out,
    row_in,
    corner_out,
    corner_in,
    surf,
    sizer,
    load_sem,
    send_sem,
    recv_sem,
    told_sem,
    other_sem,
):
    levels, rows, cols, n_lat, n_lon = sizes
    plan = Layout(rows, cols)
    groups = levels // 8
    comp = lax.axis_index("comp")
    lat = lax.axis_index("lat")
    lon = lax.axis_index("lon")
    west = lax.rem(lon + n_lon - 1, n_lon)
    east = lax.rem(lon + 1, n_lon)
    other = 1 - comp
    has = (lat > 0, lat < n_lat - 1)
    beside = (lat - 1, lat + 1)

    barrier = pltpu.get_barrier_semaphore()

    def greet(to):
        pl.semaphore_signal(barrier, inc=1, device_id=to, device_id_type=MESH)

    beside_x = (east, west)
    early = (lon == n_lon - 1, lon > 0)
    count = [flag.astype(jnp.int32) for flag in has]
    n_beside = count[0] + count[1]
    n_early = early[0].astype(jnp.int32) + early[1].astype(jnp.int32)

    def every(there, sem):
        def tell(to):
            pl.semaphore_signal(sem, inc=1, device_id=to, device_id_type=MESH)

        tell((comp, lat, there))
        tell((other, lat, there))
        for ns in (0, 1):

            @pl.when(has[ns])
            def _(ns=ns):
                tell((comp, beside[ns], there))

    for d in (0, 1):

        @pl.when(jnp.logical_not(early[d]))
        def _(d=d):
            every(beside_x[d], barrier)

    for ns in (0, 1):

        @pl.when(has[ns])
        def _(ns=ns):
            greet((comp, beside[ns], lon))

    @pl.when(comp == 0)
    def _():
        greet((other, lat, lon))

    def enter(extra):
        pl.semaphore_wait(barrier, n_beside + n_early * (2 + n_beside) + extra)
        for d in (0, 1):

            @pl.when(early[d])
            def _(d=d):
                every(beside_x[d], told_sem)

        if extra:
            pl.semaphore_signal(
                other_sem, inc=1, device_id=(other, lat, lon), device_id_type=MESH
            )

    small = (
        (push_in, push_v),
        (fill_in, fill_v),
        (vert_in, vert_v),
        (land_in, land_v),
        (match_in, match_v),
        (count_in, count_v),
    )
    first = HALO
    last = HALO + rows - 1
    loads = [
        pltpu.make_async_copy(src, dst, load_sem.at[3 + k])
        for k, (src, dst) in enumerate(small)
    ]
    for copy in loads:
        copy.start()
    for f in (PR, U, V):
        for y in range(rows):
            pltpu.make_async_copy(
                state.at[f, :, y, :], ext.at[f, first + y], load_sem.at[f]
            ).start()

    def wait_field(f):
        own = ext.at[f, pl.ds(first, rows)]
        pltpu.make_async_copy(own, own, load_sem.at[f]).wait()

    for ns in (0, 1):

        @pl.when(jnp.logical_not(has[ns]))
        def _(ns=ns):
            row_in[ns] = jnp.zeros(row_in.shape[1:], jnp.float32)
            land_y[ns] = jnp.zeros((8, cols), jnp.int32)
            for side in (0, 1):
                corner_in[side, ns] = jnp.zeros((8, cols), jnp.float32)

    present = [flag.astype(jnp.float32) for flag in has]
    lane = lax.broadcasted_iota(jnp.int32, (levels, cols), 1)
    lane8 = lax.broadcasted_iota(jnp.int32, (8, cols), 1)
    j, block = lax.rem(lane, SPAN), lane // SPAN
    j8, block8 = lax.rem(lane8, SPAN), lane8 // SPAN
    west8 = block8 < plan.half
    by_size = {levels: (j, block), 8: (j8, block8)}

    def is_own(size):
        jj, blk = by_size[size]
        return ((blk < plan.half) & (jj >= HALO)) | ((blk >= plan.half) & (jj < HALO))

    stack = lambda x: jnp.concatenate([x] * groups, axis=0)

    def coriolis(row):
        angle = (row.astype(jnp.float32) + 0.5) / (n_lat * rows) - 0.5
        return CORIOLIS * jnp.sin(math.pi * angle)

    base_row = lat * rows - HALO
    fcor = coriolis(
        lax.broadcasted_iota(jnp.int32, (rows + 2 * HALO, cols), 0) + base_row
    )
    local8 = lax.rem(block8, plan.half)
    strip_fcor = [stack(coriolis(SETS * local8 + r + base_row)) for r in range(SETS)]

    def roll(x, by):
        by = by % cols
        return pltpu.roll(x, by, 1) if by else x

    def remote(src, dst, sent, got, to):
        return pltpu.make_async_remote_copy(
            src_ref=src,
            dst_ref=dst,
            send_sem=send_sem.at[sent],
            recv_sem=recv_sem.at[got],
            device_id=to,
            device_id_type=MESH,
        )

    def side_copy(k, to):
        return remote(side_out.at[k], side_in.at[k], 0, 0, (comp, lat, to))

    sides = [side_copy(0, east), side_copy(1, west)]

    def corner_copy(ns, side):
        return remote(
            corner_out.at[ns, side],
            corner_in.at[side, 1 - ns],
            1 + ns,
            1 + (1 - ns),
            (comp, beside[ns], (east, west)[side]),
        )

    def row_copies(ns):
        its = 1 - ns
        to = (comp, beside[ns], lon)
        start = 0 if ns == 0 else rows - 8
        return [
            remote(row_out.at[ns], row_in.at[its], 1 + ns, 3 + its, to),
            remote(land_in.at[pl.ds(start, 8)], land_y.at[its], 1 + ns, 3 + its, to),
        ]

    across = [
        remote(state.at[:, 0], surf.at[k], 0, 5, (other, lat, there))
        for k, there in enumerate((lon, east, west))
    ]

    side_size = side_out.shape[1]
    row_size = row_out.shape[1] + 8

    def wait_for(sem, size):
        view = sizer.at[pl.ds(0, size)]
        pltpu.make_async_copy(view, view, sem).wait()

    @pl.when(comp == 1)
    def _():
        enter(1)
        for d in (0, 1):

            @pl.when(early[d])
            def _(d=d):
                across[1 + d].start()

        across[0].start()

    def pack(row):
        result = None
        for y in range(rows):
            d = plan.dense[y]
            turned = roll(row(y), SPAN * d + HALO)
            where = (block if turned.shape[0] == levels else block8) == d
            result = turned if result is None else jnp.where(where, turned, result)
        return result

    def pack_field(f):
        packed = pack(lambda y: ext[f, first + y])
        dense[f] = packed
        return packed

    for copy in loads[:4]:
        copy.wait()
    dry = comp == 1
    mask = jnp.where(dry, land_v[...].astype(jnp.float32), 1.0)
    spread = jnp.broadcast_to
    diag = lax.broadcasted_iota(jnp.int32, (levels, levels), 0) == lax.broadcasted_iota(
        jnp.int32, (levels, levels), 1
    )

    def per_level(ref):
        wide = spread(ref[...], (levels, levels))
        column = jnp.sum(jnp.where(diag, wide, 0.0), axis=1, keepdims=True)
        return spread(column * 0.5, (levels, cols))

    hp = per_level(push_v)
    hf = per_level(fill_v)
    vert = vert_v[...]
    vert_hi = vert.astype(jnp.bfloat16).astype(jnp.float32)
    vert_cat = jnp.concatenate([vert_hi, vert_hi, vert - vert_hi], axis=1).astype(
        jnp.bfloat16
    )

    def split(x):
        hi = x.astype(jnp.bfloat16)
        lo = (x - hi.astype(jnp.float32)).astype(jnp.bfloat16)
        return jnp.concatenate([hi, lo, hi], axis=0)

    def product(pieces):
        result = jnp.dot(
            vert_cat,
            jnp.concatenate([split(x) for x in pieces], axis=1),
            preferred_element_type=jnp.float32,
        )
        return [result[:, i * cols : (i + 1) * cols] for i in range(len(pieces))]

    low = j < HALO
    wait_field(PR)
    qp = pack_field(PR)
    wait_field(U)
    qu = pack_field(U)
    side_out[0, pl.ds(0, levels)] = jnp.where(low, qp, roll(qu, HALO))
    side_out[1, pl.ds(0, levels)] = jnp.where(low, roll(qu, -HALO), qp)
    wait_field(V)
    turn = {PR: 0, U: -2, V: 2}
    for ns in (0, 1):
        its = 1 - ns
        picked = (0, 1) if ns == 0 else (rows - 2, rows - 1)
        found = {}
        for f in (U, V, PR):
            total = jnp.zeros((8, cols), jnp.float32)
            for k, y in enumerate(picked):
                value = ext[f, first + y]
                for g in range(groups):
                    b = (SLOTS[g] + plan.corner(0, its) + 2 * k) % plan.blocks
                    piece = roll(value[8 * g : 8 * g + 8], SPAN * b + HALO + turn[f])
                    total = jnp.where(block8 == b, piece, total)
            found[f] = total
        for f in (U, V, PR):
            row_out[ns, pl.ds(ROWS * levels + 8 * f, 8)] = found[f]
        to_east = jnp.where(j8 < 2, found[U], jnp.where(j8 < 4, found[PR], found[V]))
        to_west = jnp.where(j8 < 4, found[U], jnp.where(j8 < 6, found[PR], found[V]))
        corner_out[ns, 0] = to_east
        corner_out[ns, 1] = roll(to_west, SPAN * plan.half)

    @pl.when(comp == 0)
    def _():
        enter(0)

    def send_corners(d):
        for ns in (0, 1):

            @pl.when(has[ns])
            def _(ns=ns):
                corner_copy(ns, d).start()

    for d in (0, 1):

        @pl.when(early[d])
        def _(d=d):
            send_corners(d)

    qv = pack_field(V)
    mid_level = levels // 2
    half_low = low[:mid_level]
    v_low, v_high = qv[:mid_level], qv[mid_level:]
    side_out[0, pl.ds(levels, mid_level)] = jnp.where(half_low, v_low, roll(v_high, HALO))
    side_out[1, pl.ds(levels, mid_level)] = jnp.where(half_low, roll(v_high, -HALO), v_low)
    qm = pack(lambda y: spread(mask[y : y + 1], (8, cols)))
    side_out[0, pl.ds(levels + mid_level, 8)] = qm
    side_out[1, pl.ds(levels + mid_level, 8)] = qm

    for d in (0, 1):

        @pl.when(early[d])
        def _(d=d):
            sides[d].start()

    is_first, is_last = lane == 0, lane == cols - 1

    def span_x(x):
        return jnp.where(is_last, 0.0, roll(x, -1)) - jnp.where(is_first, 0.0, roll(x, 1))

    beyond_mask = []

    def keep(e):
        if e < first:
            return beyond_mask[0][e + 8 - first : e + 9 - first]
        if e > last:
            return beyond_mask[1][e - last - 1 : e - last]
        return mask[e - first : e - first + 1]

    def force(e):
        return fcor[e : e + 1]

    def advance_v(read, store, es):
        for e in es:
            v1 = read(V, e) - hp * (read(PR, e + 1) - read(PR, e - 1)) - force(e) * read(U, e)
            store[e] = v1

    def advance_u(read, e):
        u1 = read(U, e) + force(e) * read(V, e) - hp * span_x(read(PR, e))
        return u1, read(PR, e) - hf * span_x(u1)

    def add_v(store, e, value):
        return value - hf * (store[e + 1] - store[e - 1])

    def read_one(f, e):
        return ext[f, e]

    def read_two(f, e):
        return mid[f, e]

    def write_mid(f, e, value):
        mid[f, e] = keep(e) * value

    def write_main(f, e, value):
        main[f, e - first] = keep(e) * value

    def run(read, store, write, v_rows, u_rows, p_rows, v_kept, slot):
        advance_v(read, store, v_rows)
        for e in v_kept:
            write(V, e, store[e])
        ready = {}
        for e in u_rows:
            u1, partial = advance_u(read, e)
            write(U, e, u1)
            if e in p_rows:
                ready[e] = add_v(store, e, partial)
            else:
                part[slot[e]] = partial
        for e in p_rows:
            if e not in ready:
                ready[e] = add_v(store, e, part[slot[e]])
        for e, value in zip(p_rows, product([ready[e] for e in p_rows])):
            write(PR, e, value)

    slot_one = {first: 0, first + 1: 1, last - 1: 2, last: 3}
    slot_two = {first + 2: 4, first + 3: 5, last - 3: 6, last - 2: 7}
    span = lambda a, b: list(range(a, b + 1))

    toward = (1.0, -1.0)
    edges = ((first, first + 1, first + 2), (last, last - 1, last - 2))
    advance_v(read_one, vone, span(first + 1, first + 2) + span(last - 2, last - 1))
    for ns in (0, 1):
        a, b, c = edges[ns]
        sign = toward[ns]
        partial = {}
        for e in (a, b):
            u1, partial[e] = advance_u(read_one, e)
            mid[U, e] = keep(e) * u1
            part[slot_one[e]] = partial[e]
            if e == a:
                u_edge = u1
        w = ext[V, a] - sign * (hp * ext[PR, b]) - force(a) * ext[U, a]
        sent = (
            ext[PR, a],
            w,
            partial[a] - sign * (hf * vone[b]),
            partial[b] - sign * (hf * (vone[c] - w)),
            w - force(a) * u_edge,
        )
        for k, value in enumerate(sent):
            row_out[ns, pl.ds(k * levels, levels)] = value

    for even in (0, 1):
        for ns in (even, 1 - even):

            @pl.when(has[ns] & (lax.rem(lat, 2) == even))
            def _(ns=ns):
                for copy in row_copies(ns):
                    copy.start()

    run(
        read_one,
        vone,
        write_mid,
        span(first + 3, last - 3),
        span(first + 2, last - 2),
        span(first + 2, last - 2),
        span(first + 1, last - 1),
        slot_one,
    )
    run(
        read_two,
        vtwo,
        write_main,
        span(first + 3, last - 3),
        span(first + 2, last - 2),
        span(first + 4, last - 4),
        span(first + 3, last - 3),
        slot_two,
    )

    @pl.when(n_early < 2)
    def _():
        pl.semaphore_wait(told_sem, (2 - n_early) * (2 + n_beside))

    for d in (0, 1):

        @pl.when(jnp.logical_not(early[d]))
        def _(d=d):
            sides[d].start()
            send_corners(d)

    for d in (0, 1):

        @pl.when(jnp.logical_not(early[d]) | (comp == 0))
        def _(d=d):
            across[1 + d].start()

    @pl.when(comp == 0)
    def _():
        pl.semaphore_wait(other_sem, 1)
        across[0].start()

    for ns in (0, 1):

        @pl.when(has[ns])
        def _(ns=ns):
            wait_for(recv_sem.at[3 + ns], row_size)

    for ns in (0, 1):
        covered = jnp.where(dry, land_y[ns].astype(jnp.float32), 1.0)
        beyond_mask.append(present[ns] * covered)
    def got(ns, k):
        return row_in[ns, pl.ds(k * levels, levels)]

    ready = {}
    for ns in (0, 1):
        r, r2, r3 = edges[ns]
        a, b = (r - 1, r - 2) if ns == 0 else (r + 1, r + 2)
        sign = -toward[ns]
        p_r = ext[PR, r]
        v_r = ext[V, r] - sign * (hp * (got(ns, 0) - ext[PR, r2])) - force(r) * ext[U, r]
        v_a = present[ns] * (got(ns, 1) + sign * (hp * p_r))
        vone[r] = v_r
        mid[V, r] = keep(r) * v_r
        ready[r] = part[slot_one[r]] - sign * (hf * (v_a - vone[r2]))
        ready[r2] = part[slot_one[r2]] - sign * (hf * (v_r - vone[r3]))
        ready[a] = got(ns, 2) + sign * (hf * v_r)
        ready[b] = got(ns, 3) + hf * (hp * p_r)
    for e, value in zip(ready, product(list(ready.values()))):
        mid[PR, e] = keep(e) * value
    for ns in (0, 1):
        r = edges[ns][0]
        a, b = (r - 1, r - 2) if ns == 0 else (r + 1, r + 2)
        sign = -toward[ns]
        own_part = keep(a) * (got(ns, 4) + sign * (hp * ext[PR, r]))
        vtwo[a] = present[ns] * (own_part - sign * (hp * (mid[PR, b] - mid[PR, r])))
    run(
        read_two,
        vtwo,
        write_main,
        span(first, first + 2) + span(last - 2, last),
        [first, first + 1, last - 1, last],
        span(first, first + 3) + span(last - 3, last),
        span(first, first + 2) + span(last - 2, last),
        slot_two,
    )

    own = is_own(levels)

    def place(lower, upper, rest, r, only_own):
        by = SPAN * plan.shift[r]
        jj, blk = by_size[lower.shape[0]]
        a, b = plan.span[r]
        in_west = (blk >= a) & (blk <= b)
        in_east = (blk >= plan.half + a) & (blk <= plan.half + b)
        if only_own:
            in_west, in_east = in_west & (jj >= HALO), in_east & (jj < HALO)
        return jnp.where(
            in_west,
            roll(lower, by),
            jnp.where(in_east, roll(upper, by + SPAN * plan.half), rest),
        )

    beyond_set = [plan.beyond[0][k] % SETS for k in (0, 1)]

    def place_beyond(below, above, k):
        b, t = k, plan.north + k
        size = below.shape[0]
        blk = by_size[size][1]
        both = jnp.where(blk == b, roll(below, SPAN * b + HALO), 0.0)
        both = jnp.where(blk == t, roll(above, SPAN * t + HALO), both)
        turned = roll(both, SPAN * plan.half)
        picked = jnp.where(blk < plan.half, both, turned)
        return jnp.where(is_own(size), picked, 0.0)

    zero = jnp.zeros((levels, cols), jnp.float32)
    zero8 = jnp.zeros((8, cols), jnp.float32)

    def slots_of(side, ns, k):
        return functools.reduce(
            jnp.logical_or,
            [
                block8 == (s + plan.corner(side, ns) + 2 * k) % plan.blocks
                for s in SLOTS[:groups]
            ],
        )

    def unfold(total, f, k):
        turned = [roll(total, -SPAN * (SLOTS[g] + k) - turn[f]) for g in range(groups)]
        return jnp.concatenate(turned, axis=0)

    def beyond_rows(f):
        rest = [zero] * SETS
        here = pl.ds(ROWS * levels + 8 * f, 8)
        for k in (0, 1):
            total = jnp.where(slots_of(0, 0, k), row_in[0, here], row_in[1, here])
            both = unfold(total, f, k)
            turned = roll(both, SPAN * plan.half)
            at = lax.rem(block, plan.half)
            picked = jnp.where(block < plan.half, both, turned)
            flag = ((at == k) | (at == plan.north + k)) & is_own(levels)
            rest[beyond_set[k]] = jnp.where(flag, picked, 0.0)
        return rest

    rest = [beyond_rows(f) for f in (U, V, PR)]
    rest_mask = [zero8] * SETS
    for k in (0, 1):
        rest_mask[beyond_set[k]] = place_beyond(
            spread(keep(plan.beyond[0][k]), (8, cols)),
            spread(keep(plan.beyond[1][k]), (8, cols)),
            k,
        )
    factor = [None] * SETS
    low_v, high_v = first - 1, last + 1
    for e, flag in ((low_v, present[0]), (high_v, present[1])):
        r = e % SETS
        at = local8 == e // SETS
        factor[r] = jnp.where(at, flag, 1.0 if factor[r] is None else factor[r])
    factor = [None if x is None else stack(x) for x in factor]

    def up(x):
        return [x[1], x[2], roll(x[0], -SPAN)]

    def down(x):
        return [roll(x[2], SPAN), x[0], x[1]]

    cut_low = (block >= plan.half) & (j == 0)
    cut_high = (block < plan.half) & (j == SPAN - 1)

    def strip_step(u, v, p, masks, only_own):
        def span_strip(x):
            ahead, back = roll(x, -1), roll(x, 1)
            change = jnp.where(cut_high, 0.0, ahead) - jnp.where(cut_low, 0.0, back)
            return jnp.where(own, change, 0.0) if only_own else change

        above, under = up(p), down(p)
        v1 = []
        for r in range(SETS):
            value = v[r] - hp * (above[r] - under[r]) - strip_fcor[r] * u[r]
            v1.append(value if factor[r] is None else factor[r] * value)
        u1 = [u[r] + strip_fcor[r] * v[r] - hp * span_strip(p[r]) for r in range(SETS)]
        above, under = up(v1), down(v1)
        p1 = [p[r] - hf * (span_strip(u1[r]) + above[r] - under[r]) for r in range(SETS)]
        p2 = product(p1)
        m = [stack(x) for x in masks]
        return (
            [m[r] * u1[r] for r in range(SETS)],
            [m[r] * v1[r] for r in range(SETS)],
            [m[r] * p2[r] for r in range(SETS)],
        )

    packed = [dense[f] for f in (U, V, PR)]
    strips = [
        [place(packed[f], packed[f], rest[f][r], r, True) for r in range(SETS)]
        for f in (U, V, PR)
    ]
    own_masks = [place(qm, qm, rest_mask[r], r, True) for r in range(SETS)]
    for _ in range(2):
        strips = strip_step(*strips, own_masks, True)
    for f in (U, V, PR):
        for r in range(SETS):
            edge[f, r] = strips[f][r]

    for copy in loads[4:]:
        copy.wait()
    tiles = count_v[...].astype(jnp.float32)
    match = match_v[...]
    tile = lax.broadcasted_iota(jnp.int32, match.shape, 1)

    def coef(peer):
        mine = jnp.where((tile == lon) & (match == peer), tiles, 0.0)
        theirs = jnp.where((tile == peer) & (match == lon), tiles, 0.0)
        chosen = jnp.where(dry, mine, theirs)
        total = jnp.sum(jnp.sum(chosen, axis=1, keepdims=True), axis=0, keepdims=True)
        return spread(total, (rows, cols))

    coefs = [coef(lon), coef(west), coef(east)]
    inverse = KAPPA * mask / (coefs[0] + coefs[1] + coefs[2])
    scaled = [c * inverse for c in coefs]
    for f in (U, V, PR):
        top = ext[f, pl.ds(first, rows), 0, :]
        flux[f] = -KAPPA * mask * top

    wait_for(recv_sem.at[0], 2 * side_size)
    for ns in (0, 1):

        @pl.when(has[ns])
        def _(ns=ns):
            wait_for(recv_sem.at[1 + ns], 16)

    got_w, got_e = (side_in[k, pl.ds(0, levels)] for k in (0, 1))
    vw, ve = (side_in[k, pl.ds(levels, mid_level)] for k in (0, 1))
    mw, me = (side_in[k, pl.ds(levels + mid_level, 8)] for k in (0, 1))
    lower = [None] * 3
    upper = [None] * 3
    packed = [dense[f] for f in (U, V, PR)]
    lower[PR] = jnp.where(low, got_w, packed[PR])
    upper[PR] = jnp.where(low, packed[PR], got_e)
    lower[U] = jnp.where(low, roll(got_w, -HALO), packed[U])
    upper[U] = jnp.where(low, packed[U], roll(got_e, HALO))
    lower[V] = jnp.where(
        low, jnp.concatenate([vw, roll(vw, -HALO)], axis=0), packed[V]
    )
    upper[V] = jnp.where(
        low, packed[V], jnp.concatenate([ve, roll(ve, HALO)], axis=0)
    )
    low8 = j8 < HALO
    corners = [[rest[f][r] for r in range(SETS)] for f in (U, V, PR)]
    for k in (0, 1):
        total = corner_in[0, 0]
        for side, ns in ((0, 1), (1, 0), (1, 1)):
            total = jnp.where(slots_of(side, ns, k), corner_in[side, ns], total)
        at = functools.reduce(
            jnp.logical_or,
            [
                (block == plan.corner(side, ns) + k) & (j // 2 == 1 + side)
                for side in (0, 1)
                for ns in (0, 1)
            ],
        )
        r = beyond_set[k]
        for f in (U, V, PR):
            corners[f][r] = jnp.where(at, unfold(total, f, k), corners[f][r])
    strips = [
        [place(lower[f], upper[f], corners[f][r], r, False) for r in range(SETS)]
        for f in (U, V, PR)
    ]
    lower_mask, upper_mask = jnp.where(low8, mw, qm), jnp.where(low8, qm, me)
    masks = [place(lower_mask, upper_mask, rest_mask[r], r, False) for r in range(SETS)]
    for _ in range(2):
        strips = strip_step(*strips, masks, False)
    high = j >= HALO
    for f in (U, V, PR):
        for r in range(SETS):
            change = strips[f][r] - edge[f, r]
            edge[f, r] = jnp.where(high, change, roll(change, SPAN * plan.half))

    wait_for(recv_sem.at[5], 9 * rows)
    for f in (U, V, PR):
        value = flux[f]
        for k in range(3):
            value = value + scaled[k] * surf[k, f]
        flux[f] = value

    wait_for(send_sem.at[0], 2 * side_size + 9 * rows)
    for ns in (0, 1):

        @pl.when(has[ns])
        def _(ns=ns):
            wait_for(send_sem.at[1 + ns], row_size + 16)


def finish(sizes, main, edge, flux, out, held, sem):
    levels, rows, cols = sizes
    plan = Layout(rows, cols)
    lane = lax.broadcasted_iota(jnp.int32, (levels, cols), 1)
    near = (lane < HALO) | (lane >= cols - HALO)
    top = lax.broadcasted_iota(jnp.int32, (8, cols), 0) == 0
    for y in range(rows):
        e = y + HALO
        by = (-SPAN * (e // SETS) - HALO) % cols
        for f in (U, V, PR):
            change = pltpu.roll(edge[f, e % SETS], by, 1)
            value = main[f, y] + jnp.where(near, change, 0.0)
            added = jnp.broadcast_to(flux[f, y : y + 1], (8, cols))
            held[f, y, 0:8] = value[0:8] + jnp.where(top, added, 0.0)
            held[f, y, 8:levels] = value[8:]
            pltpu.make_async_copy(held.at[f, y], out.at[f, :, y, :], sem.at[f]).start()
    for f in (U, V, PR):
        pltpu.make_async_copy(held.at[f], held.at[f], sem.at[f]).wait()


def shards(n_lat, n_lon, state, push, fill, vertical, land, match, counts):
    _, fields, levels, rows, cols = state.shape
    assert fields == 3 and levels % 16 == 0 and levels <= 32 and rows >= 16 and n_lon > 2
    f32 = jnp.float32
    any_spec = pl.BlockSpec(memory_space=pl.ANY)
    vmem_spec = pl.BlockSpec(memory_space=pltpu.VMEM)
    tall = rows + 2 * HALO
    line = (levels, cols)
    side_rows = levels + levels // 2 + 8
    main, edge, flux = pl.pallas_call(
        functools.partial(exchange, (levels, rows, cols, n_lat, n_lon)),
        out_shape=[
            pltpu.VMEM((fields, rows) + line, f32),
            pltpu.VMEM((fields, SETS) + line, f32),
            pltpu.VMEM((fields, rows, cols), f32),
        ],
        in_specs=[any_spec] * 7,
        out_specs=[vmem_spec] * 3,
        scratch_shapes=[
            pltpu.VMEM((fields, tall) + line, f32),
            pltpu.VMEM((fields, tall) + line, f32),
            pltpu.VMEM((tall,) + line, f32),
            pltpu.VMEM((tall,) + line, f32),
            pltpu.VMEM((8,) + line, f32),
            pltpu.VMEM((fields,) + line, f32),
            pltpu.VMEM(push.shape, f32),
            pltpu.VMEM(fill.shape, f32),
            pltpu.VMEM(vertical.shape[1:], f32),
            pltpu.VMEM(land.shape, jnp.int32),
            pltpu.VMEM(match.shape[:0:-1], jnp.int32),
            pltpu.VMEM(counts.shape[:0:-1], jnp.int32),
            pltpu.VMEM((2, 8, cols), jnp.int32),
            pltpu.VMEM((2, side_rows, cols), f32),
            pltpu.VMEM((2, side_rows, cols), f32),
            pltpu.VMEM((2, ROWS * levels + 24, cols), f32),
            pltpu.VMEM((2, ROWS * levels + 24, cols), f32),
            pltpu.VMEM((2, 2, 8, cols), f32),
            pltpu.VMEM((2, 2, 8, cols), f32),
            pltpu.VMEM((3, fields, rows, cols), f32),
            pltpu.VMEM((ROWS * levels + 48 + 9 * rows, cols), f32),
            pltpu.SemaphoreType.DMA((9,)),
            pltpu.SemaphoreType.DMA((3,)),
            pltpu.SemaphoreType.DMA((6,)),
            pltpu.SemaphoreType.REGULAR,
            pltpu.SemaphoreType.REGULAR,
        ],
        compiler_params=pltpu.CompilerParams(collective_id=0, has_side_effects=True),
        name="exchange",
    )(
        state[0],
        push,
        fill,
        vertical.reshape(vertical.shape[1:]),
        land,
        match[0].T,
        counts[0].T,
    )
    main, edge, flux = (
        pltpu.with_memory_space_constraint(x, pltpu.VMEM) for x in (main, edge, flux)
    )
    result = pl.pallas_call(
        functools.partial(finish, (levels, rows, cols)),
        out_shape=jax.ShapeDtypeStruct(state.shape[1:], f32),
        in_specs=[vmem_spec] * 3,
        out_specs=any_spec,
        scratch_shapes=[
            pltpu.VMEM((fields, rows) + line, f32),
            pltpu.SemaphoreType.DMA((3,)),
        ],
        name="finish",
    )(main, edge, flux)
    return result[None]


def solution(mesh):
    sizes = dict(mesh.shape)
    return jax.shard_map(
        functools.partial(shards, sizes["lat"], sizes["lon"]),
        mesh=mesh,
        in_specs=(
            P("comp", None, None, "lat", "lon"),
            P("comp", None),
            P("comp", None),
            P("comp", None, None),
            P("lat", "lon"),
            P("lat", None, None),
            P("lat", None, None),
        ),
        out_specs=P("comp", None, None, "lat", "lon"),
        check_vma=False,
    )
```

```python
import functools
import math

import jax
import jax.numpy as jnp
from jax import lax
from jax.experimental import pallas as pl
from jax.experimental.pallas import tpu as pltpu
from jax.sharding import PartitionSpec as P

KAPPA = 0.5
CORIOLIS = 0.4
MESH = pl.DeviceIdType.MESH
HALO = 4
SPAN = 8
SETS = 3
ORDER = (1, 0, 2)
SLOTS = (0, 1, 4, 5)
U, V, PR = 0, 1, 2
ROWS = 5


class Layout:
    def __init__(self, rows, cols):
        self.blocks = cols // SPAN
        self.half = self.blocks // 2
        own = range(HALO, rows + HALO)
        assert rows * SPAN == cols and rows + 2 * HALO <= SETS * self.half
        self.dense, self.shift, self.span = {}, {}, {}
        at = 0
        for r in ORDER:
            mine = [e for e in own if e % SETS == r]
            self.shift[r] = mine[0] // SETS - at
            self.span[r] = (mine[0] // SETS, mine[-1] // SETS)
            for e in mine:
                self.dense[e - HALO] = at
                at += 1
        self.beyond = ((HALO - 2, HALO - 1), (rows + HALO, rows + HALO + 1))
        self.north = self.beyond[1][0] // SETS - self.beyond[0][0] // SETS
        for k in (0, 1):
            low, high = self.beyond[0][k], self.beyond[1][k]
            assert low % SETS == high % SETS and low // SETS == k
            assert high // SETS == self.north + k
        taken = [
            (s + self.corner(side, ns)) % self.blocks
            for side in (0, 1)
            for ns in (0, 1)
            for s in SLOTS
        ]
        assert len(set(taken)) == len(taken)

    def corner(self, side, ns):
        return self.half * side + self.north * ns


def exchange(
    sizes,
    state,
    push_in,
    fill_in,
    vert_in,
    land_in,
    match_in,
    count_in,
    main,
    edge,
    flux,
    ext,
    mid,
    vone,
    vtwo,
    part,
    dense,
    strip,
    push_v,
    fill_v,
    vert_v,
    land_v,
    match_v,
    count_v,
    land_y,
    side_out,
    side_in,
    row_out,
    row_in,
    corner_out,
    corner_in,
    surf,
    sizer,
    load_sem,
    send_sem,
    recv_sem,
    told_sem,
    other_sem,
):
    levels, rows, cols, n_lat, n_lon = sizes
    plan = Layout(rows, cols)
    groups = levels // 8
    comp = lax.axis_index("comp")
    lat = lax.axis_index("lat")
    lon = lax.axis_index("lon")
    west = lax.rem(lon + n_lon - 1, n_lon)
    east = lax.rem(lon + 1, n_lon)
    other = 1 - comp
    has = (lat > 0, lat < n_lat - 1)
    beside = (lat - 1, lat + 1)

    barrier = pltpu.get_barrier_semaphore()

    def greet(to):
        pl.semaphore_signal(barrier, inc=1, device_id=to, device_id_type=MESH)

    beside_x = (east, west)
    early = (lon == n_lon - 1, lon > 0)
    count = [flag.astype(jnp.int32) for flag in has]
    n_beside = count[0] + count[1]
    n_early = early[0].astype(jnp.int32) + early[1].astype(jnp.int32)

    def every(there, sem):
        def tell(to):
            pl.semaphore_signal(sem, inc=1, device_id=to, device_id_type=MESH)

        tell((comp, lat, there))
        tell((other, lat, there))
        for ns in (0, 1):

            @pl.when(has[ns])
            def _(ns=ns):
                tell((comp, beside[ns], there))

    for d in (0, 1):

        @pl.when(jnp.logical_not(early[d]))
        def _(d=d):
            every(beside_x[d], barrier)

    for ns in (0, 1):

        @pl.when(has[ns])
        def _(ns=ns):
            greet((comp, beside[ns], lon))

    @pl.when(comp == 0)
    def _():
        greet((other, lat, lon))

    def enter(extra):
        pl.semaphore_wait(barrier, n_beside + n_early * (2 + n_beside) + extra)
        for d in (0, 1):

            @pl.when(early[d])
            def _(d=d):
                every(beside_x[d], told_sem.at[1 - d])

        if extra:
            pl.semaphore_signal(
                other_sem, inc=1, device_id=(other, lat, lon), device_id_type=MESH
            )

    small = (
        (push_in, push_v),
        (fill_in, fill_v),
        (vert_in, vert_v),
        (land_in, land_v),
        (match_in, match_v),
        (count_in, count_v),
    )
    first = HALO
    last = HALO + rows - 1
    loads = [
        pltpu.make_async_copy(src, dst, load_sem.at[3 + k])
        for k, (src, dst) in enumerate(small)
    ]
    for copy in loads:
        copy.start()
    for f in (PR, U, V):
        for y in range(rows):
            pltpu.make_async_copy(
                state.at[f, :, y, :], ext.at[f, first + y], load_sem.at[f]
            ).start()

    def wait_field(f):
        own = ext.at[f, pl.ds(first, rows)]
        pltpu.make_async_copy(own, own, load_sem.at[f]).wait()

    for ns in (0, 1):

        @pl.when(jnp.logical_not(has[ns]))
        def _(ns=ns):
            row_in[ns] = jnp.zeros(row_in.shape[1:], jnp.float32)
            land_y[ns] = jnp.zeros((8, cols), jnp.int32)
            for side in (0, 1):
                corner_in[side, ns] = jnp.zeros((8, cols), jnp.float32)

    present = [flag.astype(jnp.float32) for flag in has]
    lane = lax.broadcasted_iota(jnp.int32, (levels, cols), 1)
    lane8 = lax.broadcasted_iota(jnp.int32, (8, cols), 1)
    j, block = lax.rem(lane, SPAN), lane // SPAN
    j8, block8 = lax.rem(lane8, SPAN), lane8 // SPAN
    west8 = block8 < plan.half
    half_lane = lane[: levels // 2]
    by_size = {
        levels: (j, block),
        levels // 2: (lax.rem(half_lane, SPAN), half_lane // SPAN),
        8: (j8, block8),
    }

    def is_own(size):
        jj, blk = by_size[size]
        return ((blk < plan.half) & (jj >= HALO)) | ((blk >= plan.half) & (jj < HALO))

    stack = lambda x: jnp.concatenate([x] * groups, axis=0)

    def coriolis(row):
        angle = (row.astype(jnp.float32) + 0.5) / (n_lat * rows) - 0.5
        return CORIOLIS * jnp.sin(math.pi * angle)

    base_row = lat * rows - HALO
    fcor = coriolis(
        lax.broadcasted_iota(jnp.int32, (rows + 2 * HALO, cols), 0) + base_row
    )
    local8 = lax.rem(block8, plan.half)
    strip_fcor = [stack(coriolis(SETS * local8 + r + base_row)) for r in range(SETS)]

    def roll(x, by):
        by = by % cols
        return pltpu.roll(x, by, 1) if by else x

    def remote(src, dst, sent, got, to):
        return pltpu.make_async_remote_copy(
            src_ref=src,
            dst_ref=dst,
            send_sem=send_sem.at[sent],
            recv_sem=recv_sem.at[got],
            device_id=to,
            device_id_type=MESH,
        )

    def side_copy(k, to):
        return remote(side_out.at[k], side_in.at[k], 0, 0, (comp, lat, to))

    sides = [side_copy(0, east), side_copy(1, west)]

    def corner_copy(ns, side):
        return remote(
            corner_out.at[ns, side],
            corner_in.at[side, 1 - ns],
            1 + ns,
            1 + (1 - ns),
            (comp, beside[ns], (east, west)[side]),
        )

    def row_copies(ns):
        its = 1 - ns
        to = (comp, beside[ns], lon)
        start = 0 if ns == 0 else rows - 8
        return [
            remote(row_out.at[ns], row_in.at[its], 1 + ns, 3 + its, to),
            remote(land_in.at[pl.ds(start, 8)], land_y.at[its], 1 + ns, 3 + its, to),
        ]

    across = [
        remote(state.at[:, 0], surf.at[k], 0, 5, (other, lat, there))
        for k, there in enumerate((lon, east, west))
    ]

    side_size = side_out.shape[1]
    row_size = row_out.shape[1] + 8

    def wait_for(sem, size):
        view = sizer.at[pl.ds(0, size)]
        pltpu.make_async_copy(view, view, sem).wait()

    @pl.when(comp == 1)
    def _():
        enter(1)
        for d in (0, 1):

            @pl.when(early[d])
            def _(d=d):
                across[1 + d].start()

        across[0].start()

    def pack(row):
        result = None
        for y in range(rows):
            d = plan.dense[y]
            turned = roll(row(y), SPAN * d + HALO)
            where = (block if turned.shape[0] == levels else block8) == d
            result = turned if result is None else jnp.where(where, turned, result)
        return result

    def pack_field(f):
        packed = pack(lambda y: ext[f, first + y])
        dense[f] = packed
        return packed

    for copy in loads[:4]:
        copy.wait()
    dry = comp == 1
    mask = jnp.where(dry, land_v[...].astype(jnp.float32), 1.0)
    spread = jnp.broadcast_to
    diag = lax.broadcasted_iota(jnp.int32, (levels, levels), 0) == lax.broadcasted_iota(
        jnp.int32, (levels, levels), 1
    )

    def per_level(ref):
        wide = spread(ref[...], (levels, levels))
        column = jnp.sum(jnp.where(diag, wide, 0.0), axis=1, keepdims=True)
        return spread(column * 0.5, (levels, cols))

    hp = per_level(push_v)
    hf = per_level(fill_v)
    vert = vert_v[...]
    vert_hi = vert.astype(jnp.bfloat16).astype(jnp.float32)
    vert_cat = jnp.concatenate([vert_hi, vert_hi, vert - vert_hi], axis=1).astype(
        jnp.bfloat16
    )

    def split(x):
        hi = x.astype(jnp.bfloat16)
        lo = (x - hi.astype(jnp.float32)).astype(jnp.bfloat16)
        return jnp.concatenate([hi, lo, hi], axis=0)

    def product(pieces):
        result = jnp.dot(
            vert_cat,
            jnp.concatenate([split(x) for x in pieces], axis=1),
            preferred_element_type=jnp.float32,
        )
        return [result[:, i * cols : (i + 1) * cols] for i in range(len(pieces))]

    qm = pack(lambda y: spread(mask[y : y + 1], (8, cols)))
    low = j < HALO
    wait_field(PR)
    qp = pack_field(PR)
    wait_field(U)
    qu = pack_field(U)
    across_by = SPAN * plan.half
    u_east = jnp.where(j == 0, stack(roll(qm, -2)), qu)
    u_west = jnp.where(j == SPAN - 1, stack(roll(qm, 3)), qu)
    side_out[0, pl.ds(0, levels)] = jnp.where(low, qp, roll(u_east, HALO))
    side_out[1, pl.ds(0, levels)] = jnp.where(
        low, roll(u_west, across_by + HALO), roll(qp, across_by)
    )
    @pl.when(comp == 0)
    def _():
        enter(0)

    turn = {PR: 0, U: -2, V: 2}

    def send_corner(ns, d):
        @pl.when(has[ns])
        def _():
            corner_copy(ns, d).start()

    def corner(ns):
        its = 1 - ns
        picked = (0, 1) if ns == 0 else (rows - 2, rows - 1)
        found = {}
        for f in (U, V, PR):
            total = jnp.zeros((8, cols), jnp.float32)
            for k, y in enumerate(picked):
                value = ext[f, first + y]
                for g in range(groups):
                    b = (SLOTS[g] + plan.corner(0, its) + 2 * k) % plan.blocks
                    piece = roll(value[8 * g : 8 * g + 8], SPAN * b + HALO + turn[f])
                    total = jnp.where(block8 == b, piece, total)
            found[f] = total
        for f in (U, V, PR):
            row_out[ns, pl.ds(ROWS * levels + 8 * f, 8)] = found[f]
        to_east = jnp.where(j8 < 2, found[U], jnp.where(j8 < 4, found[PR], found[V]))
        to_west = jnp.where(j8 < 4, found[U], jnp.where(j8 < 6, found[PR], found[V]))
        corner_out[ns, 0] = to_east
        corner_out[ns, 1] = roll(to_west, across_by)
        for d in (0, 1):

            @pl.when(early[d])
            def _(d=d):
                send_corner(ns, d)

    wait_field(V)
    corner(0)
    qv = pack_field(V)
    mid_level = levels // 2
    half_low = low[:mid_level]
    v_east = jnp.where(j == 0, stack(roll(qm, -3)), qv)
    v_west = jnp.where(j == SPAN - 1, stack(roll(qm, 2)), qv)
    side_out[0, pl.ds(levels, mid_level)] = jnp.where(
        half_low, v_east[:mid_level], roll(v_east[mid_level:], HALO)
    )
    side_out[1, pl.ds(levels, mid_level)] = jnp.where(
        half_low,
        roll(v_west[mid_level:], across_by + HALO),
        roll(v_west[:mid_level], across_by),
    )

    for d in (0, 1):

        @pl.when(early[d])
        def _(d=d):
            sides[d].start()

    corner(1)


    is_first, is_last = lane == 0, lane == cols - 1

    def span_x(x):
        return jnp.where(is_last, 0.0, roll(x, -1)) - jnp.where(is_first, 0.0, roll(x, 1))

    beyond_mask = []

    def keep(e):
        if e < first:
            return beyond_mask[0][e + 8 - first : e + 9 - first]
        if e > last:
            return beyond_mask[1][e - last - 1 : e - last]
        return mask[e - first : e - first + 1]

    def force(e):
        return fcor[e : e + 1]

    def advance_v(read, store, es):
        for e in es:
            v1 = read(V, e) - hp * (read(PR, e + 1) - read(PR, e - 1)) - force(e) * read(U, e)
            store[e] = v1

    def advance_u(read, e):
        u1 = read(U, e) + force(e) * read(V, e) - hp * span_x(read(PR, e))
        return u1, read(PR, e) - hf * span_x(u1)

    def add_v(store, e, value):
        return value - hf * (store[e + 1] - store[e - 1])

    def read_one(f, e):
        return ext[f, e]

    def read_two(f, e):
        return mid[f, e]

    def write_mid(f, e, value):
        mid[f, e] = keep(e) * value

    def write_main(f, e, value):
        main[f, e - first] = keep(e) * value

    def run(read, store, write, v_rows, u_rows, p_rows, v_kept, slot):
        advance_v(read, store, v_rows)
        for e in v_kept:
            write(V, e, store[e])
        ready = {}
        for e in u_rows:
            u1, partial = advance_u(read, e)
            write(U, e, u1)
            if e in p_rows:
                ready[e] = add_v(store, e, partial)
            else:
                part[slot[e]] = partial
        for e in p_rows:
            if e not in ready:
                ready[e] = add_v(store, e, part[slot[e]])
        for e, value in zip(p_rows, product([ready[e] for e in p_rows])):
            write(PR, e, value)

    slot_one = {first: 0, first + 1: 1, last - 1: 2, last: 3}
    slot_two = {first + 2: 4, first + 3: 5, last - 3: 6, last - 2: 7}
    span = lambda a, b: list(range(a, b + 1))

    toward = (1.0, -1.0)
    edges = ((first, first + 1, first + 2), (last, last - 1, last - 2))
    advance_v(read_one, vone, span(first + 1, first + 2) + span(last - 2, last - 1))
    for ns in (0, 1):
        a, b, c = edges[ns]
        sign = toward[ns]
        partial = {}
        for e in (a, b):
            u1, partial[e] = advance_u(read_one, e)
            mid[U, e] = keep(e) * u1
            part[slot_one[e]] = partial[e]
            if e == a:
                u_edge = u1
        w = ext[V, a] - sign * (hp * ext[PR, b]) - force(a) * ext[U, a]
        sent = (
            ext[PR, a],
            w,
            partial[a] - sign * (hf * vone[b]),
            partial[b] - sign * (hf * (vone[c] - w)),
            w - force(a) * u_edge,
        )
        for k, value in enumerate(sent):
            row_out[ns, pl.ds(k * levels, levels)] = value

    for even in (0, 1):
        for ns in (even, 1 - even):

            @pl.when(has[ns] & (lax.rem(lat, 2) == even))
            def _(ns=ns):
                for copy in row_copies(ns):
                    copy.start()

    run(
        read_one,
        vone,
        write_mid,
        span(first + 3, last - 3),
        span(first + 2, last - 2),
        span(first + 2, last - 2),
        span(first + 1, last - 1),
        slot_one,
    )
    run(
        read_two,
        vtwo,
        write_main,
        span(first + 3, last - 3),
        span(first + 2, last - 2),
        span(first + 4, last - 4),
        span(first + 3, last - 3),
        slot_two,
    )

    for d in (0, 1):

        @pl.when(jnp.logical_not(early[d]))
        def _(d=d):
            pl.semaphore_wait(told_sem.at[d], 2 + n_beside)
            sides[d].start()
            for ns in (0, 1):
                send_corner(ns, d)

    for d in (0, 1):

        @pl.when(jnp.logical_not(early[d]) | (comp == 0))
        def _(d=d):
            across[1 + d].start()

    @pl.when(comp == 0)
    def _():
        pl.semaphore_wait(other_sem, 1)
        across[0].start()

    for ns in (0, 1):

        @pl.when(has[ns])
        def _(ns=ns):
            wait_for(recv_sem.at[3 + ns], row_size)

    for ns in (0, 1):
        covered = jnp.where(dry, land_y[ns].astype(jnp.float32), 1.0)
        beyond_mask.append(present[ns] * covered)
    def got(ns, k):
        return row_in[ns, pl.ds(k * levels, levels)]

    ready = {}
    for ns in (0, 1):
        r, r2, r3 = edges[ns]
        a, b = (r - 1, r - 2) if ns == 0 else (r + 1, r + 2)
        sign = -toward[ns]
        p_r = ext[PR, r]
        v_r = ext[V, r] - sign * (hp * (got(ns, 0) - ext[PR, r2])) - force(r) * ext[U, r]
        v_a = present[ns] * (got(ns, 1) + sign * (hp * p_r))
        vone[r] = v_r
        mid[V, r] = keep(r) * v_r
        ready[r] = part[slot_one[r]] - sign * (hf * (v_a - vone[r2]))
        ready[r2] = part[slot_one[r2]] - sign * (hf * (v_r - vone[r3]))
        ready[a] = got(ns, 2) + sign * (hf * v_r)
        ready[b] = got(ns, 3) + hf * (hp * p_r)
    for e, value in zip(ready, product(list(ready.values()))):
        mid[PR, e] = keep(e) * value
    for ns in (0, 1):
        r = edges[ns][0]
        a, b = (r - 1, r - 2) if ns == 0 else (r + 1, r + 2)
        sign = -toward[ns]
        own_part = keep(a) * (got(ns, 4) + sign * (hp * ext[PR, r]))
        vtwo[a] = present[ns] * (own_part - sign * (hp * (mid[PR, b] - mid[PR, r])))
    run(
        read_two,
        vtwo,
        write_main,
        span(first, first + 2) + span(last - 2, last),
        [first, first + 1, last - 1, last],
        span(first, first + 3) + span(last - 3, last),
        span(first, first + 2) + span(last - 2, last),
        slot_two,
    )

    own = is_own(levels)

    def place(packed, rest, r, by, ours):
        jj, blk = by_size[packed.shape[0]]
        a, b = plan.span[r]
        in_west = (blk >= a) & (blk <= b)
        in_east = (blk >= plan.half + a) & (blk <= plan.half + b)
        lower = jj >= HALO if ours else jj < HALO
        upper = jj < HALO if ours else jj >= HALO
        flag = (in_west & lower) | (in_east & upper)
        return jnp.where(flag, roll(packed, SPAN * plan.shift[r] + by), rest)

    beyond_set = [plan.beyond[0][k] % SETS for k in (0, 1)]

    def place_beyond(below, above, k):
        b, t = k, plan.north + k
        size = below.shape[0]
        blk = by_size[size][1]
        both = jnp.where(blk == b, roll(below, SPAN * b + HALO), 0.0)
        both = jnp.where(blk == t, roll(above, SPAN * t + HALO), both)
        turned = roll(both, SPAN * plan.half)
        picked = jnp.where(blk < plan.half, both, turned)
        return jnp.where(is_own(size), picked, 0.0)

    zero = jnp.zeros((levels, cols), jnp.float32)
    zero8 = jnp.zeros((8, cols), jnp.float32)

    def slots_of(side, ns, k):
        return functools.reduce(
            jnp.logical_or,
            [
                block8 == (s + plan.corner(side, ns) + 2 * k) % plan.blocks
                for s in SLOTS[:groups]
            ],
        )

    def unfold(total, f, k):
        turned = [roll(total, -SPAN * (SLOTS[g] + k) - turn[f]) for g in range(groups)]
        return jnp.concatenate(turned, axis=0)

    def beyond_rows(f):
        rest = [zero] * SETS
        here = pl.ds(ROWS * levels + 8 * f, 8)
        for k in (0, 1):
            total = jnp.where(slots_of(0, 0, k), row_in[0, here], row_in[1, here])
            both = unfold(total, f, k)
            turned = roll(both, SPAN * plan.half)
            at = lax.rem(block, plan.half)
            picked = jnp.where(block < plan.half, both, turned)
            flag = ((at == k) | (at == plan.north + k)) & is_own(levels)
            rest[beyond_set[k]] = jnp.where(flag, picked, 0.0)
        return rest

    rest = [beyond_rows(f) for f in (U, V, PR)]
    rest_mask = [zero8] * SETS
    for k in (0, 1):
        rest_mask[beyond_set[k]] = place_beyond(
            spread(keep(plan.beyond[0][k]), (8, cols)),
            spread(keep(plan.beyond[1][k]), (8, cols)),
            k,
        )
    factor = [None] * SETS
    low_v, high_v = first - 1, last + 1
    for e, flag in ((low_v, present[0]), (high_v, present[1])):
        r = e % SETS
        at = local8 == e // SETS
        factor[r] = jnp.where(at, flag, 1.0 if factor[r] is None else factor[r])
    factor = [None if x is None else stack(x) for x in factor]

    def up(x):
        return [x[1], x[2], roll(x[0], -SPAN)]

    def down(x):
        return [roll(x[2], SPAN), x[0], x[1]]

    cut_low = (block >= plan.half) & (j == 0)
    cut_high = (block < plan.half) & (j == SPAN - 1)

    def strip_step(u, v, p, masks, only_own):
        def span_strip(x):
            ahead, back = roll(x, -1), roll(x, 1)
            change = jnp.where(cut_high, 0.0, ahead) - jnp.where(cut_low, 0.0, back)
            return jnp.where(own, change, 0.0) if only_own else change

        above, under = up(p), down(p)
        v1 = []
        for r in range(SETS):
            value = v[r] - hp * (above[r] - under[r]) - strip_fcor[r] * u[r]
            v1.append(value if factor[r] is None else factor[r] * value)
        u1 = [u[r] + strip_fcor[r] * v[r] - hp * span_strip(p[r]) for r in range(SETS)]
        above, under = up(v1), down(v1)
        p1 = [p[r] - hf * (span_strip(u1[r]) + above[r] - under[r]) for r in range(SETS)]
        p2 = product(p1)
        m = [stack(x) for x in masks]
        return (
            [m[r] * u1[r] for r in range(SETS)],
            [m[r] * v1[r] for r in range(SETS)],
            [m[r] * p2[r] for r in range(SETS)],
        )

    low8 = j8 < HALO
    for f in (U, V, PR):
        packed = dense[f]
        packed = jnp.where(low, roll(packed, across_by), packed)
        for r in range(SETS):
            strip[f, r] = place(packed, rest[f][r], r, 0, True)
    packed = jnp.where(low8, roll(qm, across_by), qm)
    own_masks = [place(packed, rest_mask[r], r, 0, True) for r in range(SETS)]
    strips = [[strip[f, r] for r in range(SETS)] for f in (U, V, PR)]
    for _ in range(2):
        strips = strip_step(*strips, own_masks, True)
    for f in (U, V, PR):
        for r in range(SETS):
            edge[f, r] = strips[f][r]

    for copy in loads[4:]:
        copy.wait()
    tiles = count_v[...].astype(jnp.float32)
    match = match_v[...]
    tile = lax.broadcasted_iota(jnp.int32, match.shape, 1)

    def coef(peer):
        mine = jnp.where((tile == lon) & (match == peer), tiles, 0.0)
        theirs = jnp.where((tile == peer) & (match == lon), tiles, 0.0)
        chosen = jnp.where(dry, mine, theirs)
        total = jnp.sum(jnp.sum(chosen, axis=1, keepdims=True), axis=0, keepdims=True)
        return spread(total, (rows, cols))

    coefs = [coef(lon), coef(west), coef(east)]
    inverse = KAPPA * mask / (coefs[0] + coefs[1] + coefs[2])
    scaled = [c * inverse for c in coefs]
    for f in (U, V, PR):
        top = ext[f, pl.ds(first, rows), 0, :]
        flux[f] = -KAPPA * mask * top

    wait_for(recv_sem.at[0], 2 * side_size)
    for ns in (0, 1):

        @pl.when(has[ns])
        def _(ns=ns):
            wait_for(recv_sem.at[1 + ns], 16)

    got_w, got_e = (side_in[k, pl.ds(0, levels)] for k in (0, 1))
    vw, ve = (side_in[k, pl.ds(levels, mid_level)] for k in (0, 1))
    corners = [[strip[f, r] for r in range(SETS)] for f in (U, V, PR)]
    for k in (0, 1):
        total = corner_in[0, 0]
        for side, ns in ((0, 1), (1, 0), (1, 1)):
            total = jnp.where(slots_of(side, ns, k), corner_in[side, ns], total)
        at = functools.reduce(
            jnp.logical_or,
            [
                (block == plan.corner(side, ns) + k) & (j // 2 == 1 + side)
                for side in (0, 1)
                for ns in (0, 1)
            ],
        )
        r = beyond_set[k]
        for f in (U, V, PR):
            corners[f][r] = jnp.where(at, unfold(total, f, k), corners[f][r])
    p_all = jnp.where(low, got_w, got_e)
    u_all = jnp.where(low, got_e, got_w)
    v_some = jnp.where(half_low, vw, ve)
    v_rest = jnp.where(half_low, ve, vw)
    strips = [
        [place(u_all, corners[U][r], r, -HALO, False) for r in range(SETS)],
        [
            jnp.concatenate(
                [
                    place(v_some, corners[V][r][:mid_level], r, 0, False),
                    place(v_rest, corners[V][r][mid_level:], r, -HALO, False),
                ],
                axis=0,
            )
            for r in range(SETS)
        ],
        [place(p_all, corners[PR][r], r, 0, False) for r in range(SETS)],
    ]
    mask_w = jnp.where(j8 == 2, roll(got_w[:8], -2), roll(vw[:8], 3))
    mask_e = jnp.where(j8 == HALO, roll(got_e[:8], -7), roll(ve[:8], -2))
    mask_all = jnp.where(low8, mask_w, mask_e)
    masks = [place(mask_all, own_masks[r], r, 0, False) for r in range(SETS)]
    for _ in range(2):
        strips = strip_step(*strips, masks, False)
    for f in (U, V, PR):
        for r in range(SETS):
            change = strips[f][r] - edge[f, r]
            edge[f, r] = jnp.where(low, roll(change, across_by), change)

    wait_for(recv_sem.at[5], 9 * rows)
    for f in (U, V, PR):
        value = flux[f]
        for k in range(3):
            value = value + scaled[k] * surf[k, f]
        flux[f] = value

    wait_for(send_sem.at[0], 2 * side_size + 9 * rows)
    for ns in (0, 1):

        @pl.when(has[ns])
        def _(ns=ns):
            wait_for(send_sem.at[1 + ns], row_size + 16)


def finish(sizes, main, edge, flux, out, held, sem):
    levels, rows, cols = sizes
    plan = Layout(rows, cols)
    lane = lax.broadcasted_iota(jnp.int32, (levels, cols), 1)
    near = (lane < HALO) | (lane >= cols - HALO)
    top = lax.broadcasted_iota(jnp.int32, (8, cols), 0) == 0
    for y in range(rows):
        e = y + HALO
        by = -SPAN * (e // SETS) - HALO
        for f in (U, V, PR):
            change = pltpu.roll(edge[f, e % SETS], by % cols, 1)
            value = main[f, y] + jnp.where(near, change, 0.0)
            added = jnp.broadcast_to(flux[f, y : y + 1], (8, cols))
            held[f, y, 0:8] = value[0:8] + jnp.where(top, added, 0.0)
            held[f, y, 8:levels] = value[8:]
            pltpu.make_async_copy(held.at[f, y], out.at[f, :, y, :], sem.at[f]).start()
    for f in (U, V, PR):
        pltpu.make_async_copy(held.at[f], held.at[f], sem.at[f]).wait()


def shards(n_lat, n_lon, state, push, fill, vertical, land, match, counts):
    _, fields, levels, rows, cols = state.shape
    assert fields == 3 and levels % 16 == 0 and levels <= 32 and rows >= 16 and n_lon > 2
    f32 = jnp.float32
    any_spec = pl.BlockSpec(memory_space=pl.ANY)
    vmem_spec = pl.BlockSpec(memory_space=pltpu.VMEM)
    tall = rows + 2 * HALO
    line = (levels, cols)
    side_rows = levels + levels // 2
    main, edge, flux = pl.pallas_call(
        functools.partial(exchange, (levels, rows, cols, n_lat, n_lon)),
        out_shape=[
            pltpu.VMEM((fields, rows) + line, f32),
            pltpu.VMEM((fields, SETS) + line, f32),
            pltpu.VMEM((fields, rows, cols), f32),
        ],
        in_specs=[any_spec] * 7,
        out_specs=[vmem_spec] * 3,
        scratch_shapes=[
            pltpu.VMEM((fields, tall) + line, f32),
            pltpu.VMEM((fields, tall) + line, f32),
            pltpu.VMEM((tall,) + line, f32),
            pltpu.VMEM((tall,) + line, f32),
            pltpu.VMEM((8,) + line, f32),
            pltpu.VMEM((fields,) + line, f32),
            pltpu.VMEM((fields, SETS) + line, f32),
            pltpu.VMEM(push.shape, f32),
            pltpu.VMEM(fill.shape, f32),
            pltpu.VMEM(vertical.shape[1:], f32),
            pltpu.VMEM(land.shape, jnp.int32),
            pltpu.VMEM(match.shape[:0:-1], jnp.int32),
            pltpu.VMEM(counts.shape[:0:-1], jnp.int32),
            pltpu.VMEM((2, 8, cols), jnp.int32),
            pltpu.VMEM((2, side_rows, cols), f32),
            pltpu.VMEM((2, side_rows, cols), f32),
            pltpu.VMEM((2, ROWS * levels + 24, cols), f32),
            pltpu.VMEM((2, ROWS * levels + 24, cols), f32),
            pltpu.VMEM((2, 2, 8, cols), f32),
            pltpu.VMEM((2, 2, 8, cols), f32),
            pltpu.VMEM((3, fields, rows, cols), f32),
            pltpu.VMEM((ROWS * levels + 48 + 9 * rows, cols), f32),
            pltpu.SemaphoreType.DMA((9,)),
            pltpu.SemaphoreType.DMA((3,)),
            pltpu.SemaphoreType.DMA((6,)),
            pltpu.SemaphoreType.REGULAR((2,)),
            pltpu.SemaphoreType.REGULAR,
        ],
        compiler_params=pltpu.CompilerParams(collective_id=0, has_side_effects=True),
        name="exchange",
    )(
        state[0],
        push,
        fill,
        vertical.reshape(vertical.shape[1:]),
        land,
        match[0].T,
        counts[0].T,
    )
    main, edge, flux = (
        pltpu.with_memory_space_constraint(x, pltpu.VMEM) for x in (main, edge, flux)
    )
    result = pl.pallas_call(
        functools.partial(finish, (levels, rows, cols)),
        out_shape=jax.ShapeDtypeStruct(state.shape[1:], f32),
        in_specs=[vmem_spec] * 3,
        out_specs=any_spec,
        scratch_shapes=[
            pltpu.VMEM((fields, rows) + line, f32),
            pltpu.SemaphoreType.DMA((3,)),
        ],
        name="finish",
    )(main, edge, flux)
    return result[None]


def solution(mesh):
    sizes = dict(mesh.shape)
    return jax.shard_map(
        functools.partial(shards, sizes["lat"], sizes["lon"]),
        mesh=mesh,
        in_specs=(
            P("comp", None, None, "lat", "lon"),
            P("comp", None),
            P("comp", None),
            P("comp", None, None),
            P("lat", "lon"),
            P("lat", None, None),
            P("lat", None, None),
        ),
        out_specs=P("comp", None, None, "lat", "lon"),
        check_vma=False,
    )
```

```python
import functools
import math

import jax
import jax.numpy as jnp
from jax import lax
from jax.experimental import pallas as pl
from jax.experimental.pallas import tpu as pltpu
from jax.sharding import PartitionSpec as P

KAPPA = 0.5
CORIOLIS = 0.4
MESH = pl.DeviceIdType.MESH
HALO = 4
SPAN = 8
SETS = 3
ORDER = (1, 0, 2)
SLOTS = (0, 1, 4, 5)
U, V, PR = 0, 1, 2
ROWS = 5


class Layout:
    def __init__(self, rows, cols):
        self.blocks = cols // SPAN
        self.half = self.blocks // 2
        own = range(HALO, rows + HALO)
        assert rows * SPAN == cols and rows + 2 * HALO <= SETS * self.half
        self.dense, self.shift, self.span = {}, {}, {}
        at = 0
        for r in ORDER:
            mine = [e for e in own if e % SETS == r]
            self.shift[r] = mine[0] // SETS - at
            self.span[r] = (mine[0] // SETS, mine[-1] // SETS)
            for e in mine:
                self.dense[e - HALO] = at
                at += 1
        self.beyond = ((HALO - 2, HALO - 1), (rows + HALO, rows + HALO + 1))
        self.north = self.beyond[1][0] // SETS - self.beyond[0][0] // SETS
        for k in (0, 1):
            low, high = self.beyond[0][k], self.beyond[1][k]
            assert low % SETS == high % SETS and low // SETS == k
            assert high // SETS == self.north + k
        taken = [
            (s + self.corner(side, ns)) % self.blocks
            for side in (0, 1)
            for ns in (0, 1)
            for s in SLOTS
        ]
        assert len(set(taken)) == len(taken)

    def corner(self, side, ns):
        return self.half * side + self.north * ns


def exchange(
    sizes,
    state,
    push_in,
    fill_in,
    vert_in,
    land_in,
    match_in,
    count_in,
    main,
    edge,
    flux,
    ext,
    mid,
    vone,
    vtwo,
    part,
    dense,
    strip,
    push_v,
    fill_v,
    vert_v,
    land_v,
    match_v,
    count_v,
    land_y,
    side_out,
    side_in,
    row_out,
    row_in,
    corner_out,
    corner_in,
    surf,
    sizer,
    load_sem,
    send_sem,
    recv_sem,
    told_sem,
    other_sem,
):
    levels, rows, cols, n_lat, n_lon = sizes
    plan = Layout(rows, cols)
    groups = levels // 8
    comp = lax.axis_index("comp")
    lat = lax.axis_index("lat")
    lon = lax.axis_index("lon")
    west = lax.rem(lon + n_lon - 1, n_lon)
    east = lax.rem(lon + 1, n_lon)
    other = 1 - comp
    has = (lat > 0, lat < n_lat - 1)
    beside = (lat - 1, lat + 1)

    small = (
        (land_in, land_v),
        (push_in, push_v),
        (fill_in, fill_v),
        (vert_in, vert_v),
        (match_in, match_v),
        (count_in, count_v),
    )
    first = HALO
    last = HALO + rows - 1
    loads = [
        pltpu.make_async_copy(src, dst, load_sem.at[3 + k])
        for k, (src, dst) in enumerate(small)
    ]

    def load_field(f):
        for y in range(rows):
            pltpu.make_async_copy(
                state.at[f, :, y, :], ext.at[f, first + y], load_sem.at[f]
            ).start()

    loads[0].start()
    load_field(PR)

    barrier = pltpu.get_barrier_semaphore()

    def greet(to):
        pl.semaphore_signal(barrier, inc=1, device_id=to, device_id_type=MESH)

    beside_x = (east, west)
    early = (lon == n_lon - 1, lon > 0)
    soon = (early[0], early[1] & (lon < n_lon - 1))
    count = [flag.astype(jnp.int32) for flag in has]
    n_beside = count[0] + count[1]
    n_early = early[0].astype(jnp.int32) + early[1].astype(jnp.int32)

    def every(there, sem):
        def tell(to):
            pl.semaphore_signal(sem, inc=1, device_id=to, device_id_type=MESH)

        tell((comp, lat, there))
        tell((other, lat, there))
        for ns in (0, 1):

            @pl.when(has[ns])
            def _(ns=ns):
                tell((comp, beside[ns], there))

    for d in (0, 1):

        @pl.when(jnp.logical_not(early[d]))
        def _(d=d):
            every(beside_x[d], barrier)

    for ns in (0, 1):

        @pl.when(has[ns])
        def _(ns=ns):
            greet((comp, beside[ns], lon))

    @pl.when(comp == 0)
    def _():
        greet((other, lat, lon))

    def enter(extra):
        pl.semaphore_wait(barrier, n_beside + n_early * (2 + n_beside) + extra)
        for d in (0, 1):

            @pl.when(early[d])
            def _(d=d):
                every(beside_x[d], told_sem.at[1 - d])

        if extra:
            pl.semaphore_signal(
                other_sem, inc=1, device_id=(other, lat, lon), device_id_type=MESH
            )

    load_field(U)
    load_field(V)
    for copy in loads[1:]:
        copy.start()

    def wait_field(f):
        own = ext.at[f, pl.ds(first, rows)]
        pltpu.make_async_copy(own, own, load_sem.at[f]).wait()

    for ns in (0, 1):

        @pl.when(jnp.logical_not(has[ns]))
        def _(ns=ns):
            row_in[ns] = jnp.zeros(row_in.shape[1:], jnp.float32)
            land_y[ns] = jnp.zeros((8, cols), jnp.int32)
            for side in (0, 1):
                corner_in[side, ns] = jnp.zeros((8, cols), jnp.float32)

    present = [flag.astype(jnp.float32) for flag in has]
    lane = lax.broadcasted_iota(jnp.int32, (levels, cols), 1)
    lane8 = lax.broadcasted_iota(jnp.int32, (8, cols), 1)
    j, block = lax.rem(lane, SPAN), lane // SPAN
    j8, block8 = lax.rem(lane8, SPAN), lane8 // SPAN
    west8 = block8 < plan.half
    half_lane = lane[: levels // 2]
    by_size = {
        levels: (j, block),
        levels // 2: (lax.rem(half_lane, SPAN), half_lane // SPAN),
        8: (j8, block8),
    }

    def is_own(size):
        jj, blk = by_size[size]
        return ((blk < plan.half) & (jj >= HALO)) | ((blk >= plan.half) & (jj < HALO))

    stack = lambda x: jnp.concatenate([x] * groups, axis=0)

    def coriolis(row):
        angle = (row.astype(jnp.float32) + 0.5) / (n_lat * rows) - 0.5
        return CORIOLIS * jnp.sin(math.pi * angle)

    base_row = lat * rows - HALO
    fcor = coriolis(
        lax.broadcasted_iota(jnp.int32, (rows + 2 * HALO, cols), 0) + base_row
    )
    local8 = lax.rem(block8, plan.half)
    strip_fcor = [stack(coriolis(SETS * local8 + r + base_row)) for r in range(SETS)]

    def roll(x, by):
        by = by % cols
        return pltpu.roll(x, by, 1) if by else x

    def remote(src, dst, sent, got, to):
        return pltpu.make_async_remote_copy(
            src_ref=src,
            dst_ref=dst,
            send_sem=send_sem.at[sent],
            recv_sem=recv_sem.at[got],
            device_id=to,
            device_id_type=MESH,
        )

    def side_copies(k, to):
        return [
            remote(
                side_out.at[k, pl.ds(start, size)],
                side_in.at[k, pl.ds(start, size)],
                0,
                0,
                (comp, lat, to),
            )
            for start, size in ((0, levels), (levels, levels // 2))
        ]

    sides = [side_copies(0, east), side_copies(1, west)]

    def corner_copy(ns, side):
        return remote(
            corner_out.at[ns, side],
            corner_in.at[side, 1 - ns],
            1 + ns,
            1 + (1 - ns),
            (comp, beside[ns], (east, west)[side]),
        )

    def row_copies(ns):
        its = 1 - ns
        to = (comp, beside[ns], lon)
        start = 0 if ns == 0 else rows - 8
        return [
            remote(row_out.at[ns], row_in.at[its], 1 + ns, 3 + its, to),
            remote(land_in.at[pl.ds(start, 8)], land_y.at[its], 1 + ns, 3 + its, to),
        ]

    across = [
        remote(state.at[:, 0], surf.at[k], 0, 5, (other, lat, there))
        for k, there in enumerate((lon, east, west))
    ]

    side_size = side_out.shape[1]
    row_size = row_out.shape[1] + 8

    def wait_for(sem, size):
        view = sizer.at[pl.ds(0, size)]
        pltpu.make_async_copy(view, view, sem).wait()

    @pl.when(comp == 1)
    def _():
        enter(1)
        for d in (0, 1):

            @pl.when(soon[d])
            def _(d=d):
                across[1 + d].start()

        across[0].start()

    def pack(row):
        result = None
        for y in range(rows):
            d = plan.dense[y]
            turned = roll(row(y), SPAN * d + HALO)
            where = (block if turned.shape[0] == levels else block8) == d
            result = turned if result is None else jnp.where(where, turned, result)
        return result

    def pack_field(f):
        packed = pack(lambda y: ext[f, first + y])
        dense[f] = packed
        return packed

    loads[0].wait()
    dry = comp == 1
    mask = jnp.where(dry, land_v[...].astype(jnp.float32), 1.0)
    spread = jnp.broadcast_to
    qm = pack(lambda y: spread(mask[y : y + 1], (8, cols)))
    low = j < HALO
    wait_field(PR)
    qp = pack_field(PR)
    wait_field(U)
    qu = pack_field(U)
    across_by = SPAN * plan.half
    u_east = jnp.where(j == 0, stack(roll(qm, -2)), qu)
    u_west = jnp.where(j == SPAN - 1, stack(roll(qm, 3)), qu)
    side_out[0, pl.ds(0, levels)] = jnp.where(low, qp, roll(u_east, HALO))
    side_out[1, pl.ds(0, levels)] = jnp.where(
        low, roll(u_west, across_by + HALO), roll(qp, across_by)
    )
    @pl.when(comp == 0)
    def _():
        enter(0)

    turn = {PR: 0, U: -2, V: 2}

    def send_corner(ns, d):
        @pl.when(has[ns])
        def _():
            corner_copy(ns, d).start()

    def corner(ns):
        its = 1 - ns
        picked = (0, 1) if ns == 0 else (rows - 2, rows - 1)
        found = {}
        for f in (U, V, PR):
            total = jnp.zeros((8, cols), jnp.float32)
            for k, y in enumerate(picked):
                value = ext[f, first + y]
                for g in range(groups):
                    b = (SLOTS[g] + plan.corner(0, its) + 2 * k) % plan.blocks
                    piece = roll(value[8 * g : 8 * g + 8], SPAN * b + HALO + turn[f])
                    total = jnp.where(block8 == b, piece, total)
            found[f] = total
        for f in (U, V, PR):
            row_out[ns, pl.ds(ROWS * levels + 8 * f, 8)] = found[f]
        to_east = jnp.where(j8 < 2, found[U], jnp.where(j8 < 4, found[PR], found[V]))
        to_west = jnp.where(j8 < 4, found[U], jnp.where(j8 < 6, found[PR], found[V]))
        corner_out[ns, 0] = to_east
        corner_out[ns, 1] = roll(to_west, across_by)
        for d in (0, 1):

            @pl.when(soon[d])
            def _(d=d):
                send_corner(ns, d)

    for d in (0, 1):

        @pl.when(soon[d])
        def _(d=d):
            sides[d][0].start()

    wait_field(V)

    @pl.when(has[0])
    def _():
        corner(0)

    qv = pack_field(V)
    mid_level = levels // 2
    half_low = low[:mid_level]
    v_east = jnp.where(j == 0, stack(roll(qm, -3)), qv)
    v_west = jnp.where(j == SPAN - 1, stack(roll(qm, 2)), qv)
    side_out[0, pl.ds(levels, mid_level)] = jnp.where(
        half_low, v_east[:mid_level], roll(v_east[mid_level:], HALO)
    )
    side_out[1, pl.ds(levels, mid_level)] = jnp.where(
        half_low,
        roll(v_west[mid_level:], across_by + HALO),
        roll(v_west[:mid_level], across_by),
    )

    for d in (0, 1):

        @pl.when(soon[d])
        def _(d=d):
            sides[d][1].start()

    @pl.when(has[1])
    def _():
        corner(1)

    for copy in loads[1:4]:
        copy.wait()

    diag = lax.broadcasted_iota(jnp.int32, (levels, levels), 0) == lax.broadcasted_iota(
        jnp.int32, (levels, levels), 1
    )

    def per_level(ref):
        wide = spread(ref[...], (levels, levels))
        column = jnp.sum(jnp.where(diag, wide, 0.0), axis=1, keepdims=True)
        return spread(column * 0.5, (levels, cols))

    hp = per_level(push_v)
    hf = per_level(fill_v)
    vert = vert_v[...]
    vert_hi = vert.astype(jnp.bfloat16).astype(jnp.float32)
    vert_cat = jnp.concatenate([vert_hi, vert_hi, vert - vert_hi], axis=1).astype(
        jnp.bfloat16
    )

    def split(x):
        hi = x.astype(jnp.bfloat16)
        lo = (x - hi.astype(jnp.float32)).astype(jnp.bfloat16)
        return jnp.concatenate([hi, lo, hi], axis=0)

    def product(pieces):
        result = jnp.dot(
            vert_cat,
            jnp.concatenate([split(x) for x in pieces], axis=1),
            preferred_element_type=jnp.float32,
        )
        return [result[:, i * cols : (i + 1) * cols] for i in range(len(pieces))]


    is_first, is_last = lane == 0, lane == cols - 1

    def span_x(x):
        return jnp.where(is_last, 0.0, roll(x, -1)) - jnp.where(is_first, 0.0, roll(x, 1))

    beyond_mask = []

    def keep(e):
        if e < first:
            return beyond_mask[0][e + 8 - first : e + 9 - first]
        if e > last:
            return beyond_mask[1][e - last - 1 : e - last]
        return mask[e - first : e - first + 1]

    def force(e):
        return fcor[e : e + 1]

    def advance_v(read, store, es):
        for e in es:
            v1 = read(V, e) - hp * (read(PR, e + 1) - read(PR, e - 1)) - force(e) * read(U, e)
            store[e] = v1

    def advance_u(read, e):
        u1 = read(U, e) + force(e) * read(V, e) - hp * span_x(read(PR, e))
        return u1, read(PR, e) - hf * span_x(u1)

    def add_v(store, e, value):
        return value - hf * (store[e + 1] - store[e - 1])

    def read_one(f, e):
        return ext[f, e]

    def read_two(f, e):
        return mid[f, e]

    def write_mid(f, e, value):
        mid[f, e] = keep(e) * value

    def write_main(f, e, value):
        main[f, e - first] = keep(e) * value

    def run(read, store, write, v_rows, u_rows, p_rows, v_kept, slot):
        advance_v(read, store, v_rows)
        for e in v_kept:
            write(V, e, store[e])
        ready = {}
        for e in u_rows:
            u1, partial = advance_u(read, e)
            write(U, e, u1)
            if e in p_rows:
                ready[e] = add_v(store, e, partial)
            else:
                part[slot[e]] = partial
        for e in p_rows:
            if e not in ready:
                ready[e] = add_v(store, e, part[slot[e]])
        for e, value in zip(p_rows, product([ready[e] for e in p_rows])):
            write(PR, e, value)

    slot_one = {first: 0, first + 1: 1, last - 1: 2, last: 3}
    slot_two = {first + 2: 4, first + 3: 5, last - 3: 6, last - 2: 7}
    span = lambda a, b: list(range(a, b + 1))

    toward = (1.0, -1.0)
    edges = ((first, first + 1, first + 2), (last, last - 1, last - 2))
    advance_v(read_one, vone, span(first + 1, first + 2) + span(last - 2, last - 1))
    for ns in (0, 1):
        a, b, c = edges[ns]
        sign = toward[ns]
        partial = {}
        for e in (a, b):
            u1, partial[e] = advance_u(read_one, e)
            mid[U, e] = keep(e) * u1
            part[slot_one[e]] = partial[e]
            if e == a:
                u_edge = u1
        w = ext[V, a] - sign * (hp * ext[PR, b]) - force(a) * ext[U, a]
        sent = (
            ext[PR, a],
            w,
            partial[a] - sign * (hf * vone[b]),
            partial[b] - sign * (hf * (vone[c] - w)),
            w - force(a) * u_edge,
        )
        for k, value in enumerate(sent):
            row_out[ns, pl.ds(k * levels, levels)] = value

    def send_rows():
        for even in (0, 1):
            for ns in (even, 1 - even):

                @pl.when(has[ns] & (lax.rem(lat, 2) == even))
                def _(ns=ns):
                    for copy in row_copies(ns):
                        copy.start()

    @pl.when(lon < n_lon - 1)
    def _():
        send_rows()

    run(
        read_one,
        vone,
        write_mid,
        span(first + 3, last - 3),
        span(first + 2, last - 2),
        span(first + 2, last - 2),
        span(first + 1, last - 1),
        slot_one,
    )
    @pl.when(lon == n_lon - 1)
    def _():
        send_rows()

    run(
        read_two,
        vtwo,
        write_main,
        span(first + 3, last - 3),
        span(first + 2, last - 2),
        span(first + 4, last - 4),
        span(first + 3, last - 3),
        slot_two,
    )

    for d in (0, 1):

        @pl.when(jnp.logical_not(early[d]))
        def _(d=d):
            pl.semaphore_wait(told_sem.at[d], 2 + n_beside)

        @pl.when(jnp.logical_not(soon[d]))
        def _(d=d):
            for copy in sides[d]:
                copy.start()
            for ns in (0, 1):
                send_corner(ns, d)

    for d in (0, 1):

        @pl.when(jnp.logical_not(soon[d]) | (comp == 0))
        def _(d=d):
            across[1 + d].start()

    @pl.when(comp == 0)
    def _():
        pl.semaphore_wait(other_sem, 1)
        across[0].start()

    for ns in (0, 1):

        @pl.when(has[ns])
        def _(ns=ns):
            wait_for(recv_sem.at[3 + ns], row_size)

    for ns in (0, 1):
        covered = jnp.where(dry, land_y[ns].astype(jnp.float32), 1.0)
        beyond_mask.append(present[ns] * covered)
    def got(ns, k):
        return row_in[ns, pl.ds(k * levels, levels)]

    ready = {}
    for ns in (0, 1):
        r, r2, r3 = edges[ns]
        a, b = (r - 1, r - 2) if ns == 0 else (r + 1, r + 2)
        sign = -toward[ns]
        p_r = ext[PR, r]
        v_r = ext[V, r] - sign * (hp * (got(ns, 0) - ext[PR, r2])) - force(r) * ext[U, r]
        v_a = present[ns] * (got(ns, 1) + sign * (hp * p_r))
        vone[r] = v_r
        mid[V, r] = keep(r) * v_r
        ready[r] = part[slot_one[r]] - sign * (hf * (v_a - vone[r2]))
        ready[r2] = part[slot_one[r2]] - sign * (hf * (v_r - vone[r3]))
        ready[a] = got(ns, 2) + sign * (hf * v_r)
        ready[b] = got(ns, 3) + hf * (hp * p_r)
    for e, value in zip(ready, product(list(ready.values()))):
        mid[PR, e] = keep(e) * value
    for ns in (0, 1):
        r = edges[ns][0]
        a, b = (r - 1, r - 2) if ns == 0 else (r + 1, r + 2)
        sign = -toward[ns]
        own_part = keep(a) * (got(ns, 4) + sign * (hp * ext[PR, r]))
        vtwo[a] = present[ns] * (own_part - sign * (hp * (mid[PR, b] - mid[PR, r])))
    run(
        read_two,
        vtwo,
        write_main,
        span(first, first + 2) + span(last - 2, last),
        [first, first + 1, last - 1, last],
        span(first, first + 3) + span(last - 3, last),
        span(first, first + 2) + span(last - 2, last),
        slot_two,
    )

    own = is_own(levels)

    def place(packed, rest, r, by, ours):
        jj, blk = by_size[packed.shape[0]]
        a, b = plan.span[r]
        in_west = (blk >= a) & (blk <= b)
        in_east = (blk >= plan.half + a) & (blk <= plan.half + b)
        lower = jj >= HALO if ours else jj < HALO
        upper = jj < HALO if ours else jj >= HALO
        flag = (in_west & lower) | (in_east & upper)
        return jnp.where(flag, roll(packed, SPAN * plan.shift[r] + by), rest)

    beyond_set = [plan.beyond[0][k] % SETS for k in (0, 1)]

    def place_beyond(below, above, k):
        b, t = k, plan.north + k
        size = below.shape[0]
        blk = by_size[size][1]
        both = jnp.where(blk == b, roll(below, SPAN * b + HALO), 0.0)
        both = jnp.where(blk == t, roll(above, SPAN * t + HALO), both)
        turned = roll(both, SPAN * plan.half)
        picked = jnp.where(blk < plan.half, both, turned)
        return jnp.where(is_own(size), picked, 0.0)

    zero = jnp.zeros((levels, cols), jnp.float32)
    zero8 = jnp.zeros((8, cols), jnp.float32)

    def slots_of(side, ns, k):
        return functools.reduce(
            jnp.logical_or,
            [
                block8 == (s + plan.corner(side, ns) + 2 * k) % plan.blocks
                for s in SLOTS[:groups]
            ],
        )

    def unfold(total, f, k):
        turned = [roll(total, -SPAN * (SLOTS[g] + k) - turn[f]) for g in range(groups)]
        return jnp.concatenate(turned, axis=0)

    def beyond_rows(f):
        rest = [zero] * SETS
        here = pl.ds(ROWS * levels + 8 * f, 8)
        for k in (0, 1):
            total = jnp.where(slots_of(0, 0, k), row_in[0, here], row_in[1, here])
            both = unfold(total, f, k)
            turned = roll(both, SPAN * plan.half)
            at = lax.rem(block, plan.half)
            picked = jnp.where(block < plan.half, both, turned)
            flag = ((at == k) | (at == plan.north + k)) & is_own(levels)
            rest[beyond_set[k]] = jnp.where(flag, picked, 0.0)
        return rest

    rest = [beyond_rows(f) for f in (U, V, PR)]
    rest_mask = [zero8] * SETS
    for k in (0, 1):
        rest_mask[beyond_set[k]] = place_beyond(
            spread(keep(plan.beyond[0][k]), (8, cols)),
            spread(keep(plan.beyond[1][k]), (8, cols)),
            k,
        )
    factor = [None] * SETS
    low_v, high_v = first - 1, last + 1
    for e, flag in ((low_v, present[0]), (high_v, present[1])):
        r = e % SETS
        at = local8 == e // SETS
        factor[r] = jnp.where(at, flag, 1.0 if factor[r] is None else factor[r])
    factor = [None if x is None else stack(x) for x in factor]

    def up(x):
        return [x[1], x[2], roll(x[0], -SPAN)]

    def down(x):
        return [roll(x[2], SPAN), x[0], x[1]]

    cut_low = (block >= plan.half) & (j == 0)
    cut_high = (block < plan.half) & (j == SPAN - 1)

    def strip_step(u, v, p, masks, only_own):
        def span_strip(x):
            ahead, back = roll(x, -1), roll(x, 1)
            change = jnp.where(cut_high, 0.0, ahead) - jnp.where(cut_low, 0.0, back)
            return jnp.where(own, change, 0.0) if only_own else change

        above, under = up(p), down(p)
        v1 = []
        for r in range(SETS):
            value = v[r] - hp * (above[r] - under[r]) - strip_fcor[r] * u[r]
            v1.append(value if factor[r] is None else factor[r] * value)
        u1 = [u[r] + strip_fcor[r] * v[r] - hp * span_strip(p[r]) for r in range(SETS)]
        above, under = up(v1), down(v1)
        p1 = [p[r] - hf * (span_strip(u1[r]) + above[r] - under[r]) for r in range(SETS)]
        p2 = product(p1)
        m = [stack(x) for x in masks]
        return (
            [m[r] * u1[r] for r in range(SETS)],
            [m[r] * v1[r] for r in range(SETS)],
            [m[r] * p2[r] for r in range(SETS)],
        )

    low8 = j8 < HALO
    for f in (U, V, PR):
        packed = dense[f]
        packed = jnp.where(low, roll(packed, across_by), packed)
        for r in range(SETS):
            strip[f, r] = place(packed, rest[f][r], r, 0, True)
    packed = jnp.where(low8, roll(qm, across_by), qm)
    own_masks = [place(packed, rest_mask[r], r, 0, True) for r in range(SETS)]
    strips = [[strip[f, r] for r in range(SETS)] for f in (U, V, PR)]
    for _ in range(2):
        strips = strip_step(*strips, own_masks, True)
    for f in (U, V, PR):
        for r in range(SETS):
            edge[f, r] = strips[f][r]

    for copy in loads[4:]:
        copy.wait()
    tiles = count_v[...].astype(jnp.float32)
    match = match_v[...]
    tile = lax.broadcasted_iota(jnp.int32, match.shape, 1)

    def coef(peer):
        mine = jnp.where((tile == lon) & (match == peer), tiles, 0.0)
        theirs = jnp.where((tile == peer) & (match == lon), tiles, 0.0)
        chosen = jnp.where(dry, mine, theirs)
        total = jnp.sum(jnp.sum(chosen, axis=1, keepdims=True), axis=0, keepdims=True)
        return spread(total, (rows, cols))

    coefs = [coef(lon), coef(west), coef(east)]
    inverse = KAPPA * mask / (coefs[0] + coefs[1] + coefs[2])
    scaled = [c * inverse for c in coefs]
    for f in (U, V, PR):
        top = ext[f, pl.ds(first, rows), 0, :]
        flux[f] = -KAPPA * mask * top

    wait_for(recv_sem.at[0], 2 * side_size)
    for ns in (0, 1):

        @pl.when(has[ns])
        def _(ns=ns):
            wait_for(recv_sem.at[1 + ns], 16)

    got_w, got_e = (side_in[k, pl.ds(0, levels)] for k in (0, 1))
    vw, ve = (side_in[k, pl.ds(levels, mid_level)] for k in (0, 1))
    corners = [[strip[f, r] for r in range(SETS)] for f in (U, V, PR)]
    for k in (0, 1):
        total = corner_in[0, 0]
        for side, ns in ((0, 1), (1, 0), (1, 1)):
            total = jnp.where(slots_of(side, ns, k), corner_in[side, ns], total)
        at = functools.reduce(
            jnp.logical_or,
            [
                (block == plan.corner(side, ns) + k) & (j // 2 == 1 + side)
                for side in (0, 1)
                for ns in (0, 1)
            ],
        )
        r = beyond_set[k]
        for f in (U, V, PR):
            corners[f][r] = jnp.where(at, unfold(total, f, k), corners[f][r])
    p_all = jnp.where(low, got_w, got_e)
    u_all = jnp.where(low, got_e, got_w)
    v_some = jnp.where(half_low, vw, ve)
    v_rest = jnp.where(half_low, ve, vw)
    strips = [
        [place(u_all, corners[U][r], r, -HALO, False) for r in range(SETS)],
        [
            jnp.concatenate(
                [
                    place(v_some, corners[V][r][:mid_level], r, 0, False),
                    place(v_rest, corners[V][r][mid_level:], r, -HALO, False),
                ],
                axis=0,
            )
            for r in range(SETS)
        ],
        [place(p_all, corners[PR][r], r, 0, False) for r in range(SETS)],
    ]
    mask_w = jnp.where(j8 == 2, roll(got_w[:8], -2), roll(vw[:8], 3))
    mask_e = jnp.where(j8 == HALO, roll(got_e[:8], -7), roll(ve[:8], -2))
    mask_all = jnp.where(low8, mask_w, mask_e)
    masks = [place(mask_all, own_masks[r], r, 0, False) for r in range(SETS)]
    for _ in range(2):
        strips = strip_step(*strips, masks, False)
    for f in (U, V, PR):
        for r in range(SETS):
            change = strips[f][r] - edge[f, r]
            edge[f, r] = jnp.where(low, roll(change, across_by), change)

    wait_for(recv_sem.at[5], 9 * rows)
    for f in (U, V, PR):
        value = flux[f]
        for k in range(3):
            value = value + scaled[k] * surf[k, f]
        flux[f] = value

    wait_for(send_sem.at[0], 2 * side_size + 9 * rows)
    for ns in (0, 1):

        @pl.when(has[ns])
        def _(ns=ns):
            wait_for(send_sem.at[1 + ns], row_size + 16)


def finish(sizes, main, edge, flux, out, held, sem):
    levels, rows, cols = sizes
    plan = Layout(rows, cols)
    lane = lax.broadcasted_iota(jnp.int32, (levels, cols), 1)
    near = (lane < HALO) | (lane >= cols - HALO)
    top = lax.broadcasted_iota(jnp.int32, (8, cols), 0) == 0
    for y in range(rows):
        e = y + HALO
        by = -SPAN * (e // SETS) - HALO
        for f in (U, V, PR):
            change = pltpu.roll(edge[f, e % SETS], by % cols, 1)
            value = main[f, y] + jnp.where(near, change, 0.0)
            added = jnp.broadcast_to(flux[f, y : y + 1], (8, cols))
            held[f, y, 0:8] = value[0:8] + jnp.where(top, added, 0.0)
            held[f, y, 8:levels] = value[8:]
            pltpu.make_async_copy(held.at[f, y], out.at[f, :, y, :], sem.at[f]).start()
    for f in (U, V, PR):
        pltpu.make_async_copy(held.at[f], held.at[f], sem.at[f]).wait()


def shards(n_lat, n_lon, state, push, fill, vertical, land, match, counts):
    _, fields, levels, rows, cols = state.shape
    assert fields == 3 and levels % 16 == 0 and levels <= 32 and rows >= 16 and n_lon > 2
    f32 = jnp.float32
    any_spec = pl.BlockSpec(memory_space=pl.ANY)
    vmem_spec = pl.BlockSpec(memory_space=pltpu.VMEM)
    tall = rows + 2 * HALO
    line = (levels, cols)
    side_rows = levels + levels // 2
    main, edge, flux = pl.pallas_call(
        functools.partial(exchange, (levels, rows, cols, n_lat, n_lon)),
        out_shape=[
            pltpu.VMEM((fields, rows) + line, f32),
            pltpu.VMEM((fields, SETS) + line, f32),
            pltpu.VMEM((fields, rows, cols), f32),
        ],
        in_specs=[any_spec] * 7,
        out_specs=[vmem_spec] * 3,
        scratch_shapes=[
            pltpu.VMEM((fields, tall) + line, f32),
            pltpu.VMEM((fields, tall) + line, f32),
            pltpu.VMEM((tall,) + line, f32),
            pltpu.VMEM((tall,) + line, f32),
            pltpu.VMEM((8,) + line, f32),
            pltpu.VMEM((fields,) + line, f32),
            pltpu.VMEM((fields, SETS) + line, f32),
            pltpu.VMEM(push.shape, f32),
            pltpu.VMEM(fill.shape, f32),
            pltpu.VMEM(vertical.shape[1:], f32),
            pltpu.VMEM(land.shape, jnp.int32),
            pltpu.VMEM(match.shape[:0:-1], jnp.int32),
            pltpu.VMEM(counts.shape[:0:-1], jnp.int32),
            pltpu.VMEM((2, 8, cols), jnp.int32),
            pltpu.VMEM((2, side_rows, cols), f32),
            pltpu.VMEM((2, side_rows, cols), f32),
            pltpu.VMEM((2, ROWS * levels + 24, cols), f32),
            pltpu.VMEM((2, ROWS * levels + 24, cols), f32),
            pltpu.VMEM((2, 2, 8, cols), f32),
            pltpu.VMEM((2, 2, 8, cols), f32),
            pltpu.VMEM((3, fields, rows, cols), f32),
            pltpu.VMEM((ROWS * levels + 48 + 9 * rows, cols), f32),
            pltpu.SemaphoreType.DMA((9,)),
            pltpu.SemaphoreType.DMA((3,)),
            pltpu.SemaphoreType.DMA((6,)),
            pltpu.SemaphoreType.REGULAR((2,)),
            pltpu.SemaphoreType.REGULAR,
        ],
        compiler_params=pltpu.CompilerParams(collective_id=0, has_side_effects=True),
        name="exchange",
    )(
        state[0],
        push,
        fill,
        vertical.reshape(vertical.shape[1:]),
        land,
        match[0].T,
        counts[0].T,
    )
    main, edge, flux = (
        pltpu.with_memory_space_constraint(x, pltpu.VMEM) for x in (main, edge, flux)
    )
    result = pl.pallas_call(
        functools.partial(finish, (levels, rows, cols)),
        out_shape=jax.ShapeDtypeStruct(state.shape[1:], f32),
        in_specs=[vmem_spec] * 3,
        out_specs=any_spec,
        scratch_shapes=[
            pltpu.VMEM((fields, rows) + line, f32),
            pltpu.SemaphoreType.DMA((3,)),
        ],
        name="finish",
    )(main, edge, flux)
    return result[None]


def solution(mesh):
    sizes = dict(mesh.shape)
    return jax.shard_map(
        functools.partial(shards, sizes["lat"], sizes["lon"]),
        mesh=mesh,
        in_specs=(
            P("comp", None, None, "lat", "lon"),
            P("comp", None),
            P("comp", None),
            P("comp", None, None),
            P("lat", "lon"),
            P("lat", None, None),
            P("lat", None, None),
        ),
        out_specs=P("comp", None, None, "lat", "lon"),
        check_vma=False,
    )
```

```python
import functools
import math

import jax
import jax.numpy as jnp
from jax import lax
from jax.experimental import pallas as pl
from jax.experimental.pallas import tpu as pltpu
from jax.sharding import PartitionSpec as P

KAPPA = 0.5
CORIOLIS = 0.4
MESH = pl.DeviceIdType.MESH
HALO = 4
SPAN = 8
SETS = 3
ORDER = (1, 0, 2)
SLOTS = (0, 1, 4, 5)
U, V, PR = 0, 1, 2
ROWS = 5


class Layout:
    def __init__(self, rows, cols):
        self.blocks = cols // SPAN
        self.half = self.blocks // 2
        own = range(HALO, rows + HALO)
        assert rows * SPAN == cols and rows + 2 * HALO <= SETS * self.half
        self.dense, self.shift, self.span = {}, {}, {}
        at = 0
        for r in ORDER:
            mine = [e for e in own if e % SETS == r]
            self.shift[r] = mine[0] // SETS - at
            self.span[r] = (mine[0] // SETS, mine[-1] // SETS)
            for e in mine:
                self.dense[e - HALO] = at
                at += 1
        self.beyond = ((HALO - 2, HALO - 1), (rows + HALO, rows + HALO + 1))
        self.north = self.beyond[1][0] // SETS - self.beyond[0][0] // SETS
        for k in (0, 1):
            low, high = self.beyond[0][k], self.beyond[1][k]
            assert low % SETS == high % SETS and low // SETS == k
            assert high // SETS == self.north + k
        taken = [
            (s + self.corner(side, ns)) % self.blocks
            for side in (0, 1)
            for ns in (0, 1)
            for s in SLOTS
        ]
        assert len(set(taken)) == len(taken)

    def corner(self, side, ns):
        return self.half * side + self.north * ns


def exchange(
    sizes,
    state,
    push_in,
    fill_in,
    vert_in,
    land_in,
    match_in,
    count_in,
    main,
    edge,
    flux,
    ext,
    mid,
    vone,
    vtwo,
    part,
    dense,
    strip,
    push_v,
    fill_v,
    vert_v,
    land_v,
    match_v,
    count_v,
    land_y,
    side_out,
    side_in,
    row_out,
    row_in,
    corner_out,
    corner_in,
    surf,
    sizer,
    load_sem,
    send_sem,
    recv_sem,
    told_sem,
    other_sem,
):
    levels, rows, cols, n_lat, n_lon = sizes
    plan = Layout(rows, cols)
    groups = levels // 8
    comp = lax.axis_index("comp")
    lat = lax.axis_index("lat")
    lon = lax.axis_index("lon")
    west = lax.rem(lon + n_lon - 1, n_lon)
    east = lax.rem(lon + 1, n_lon)
    other = 1 - comp
    has = (lat > 0, lat < n_lat - 1)
    beside = (lat - 1, lat + 1)

    small = (
        (land_in, land_v),
        (push_in, push_v),
        (fill_in, fill_v),
        (vert_in, vert_v),
        (match_in, match_v),
        (count_in, count_v),
    )
    first = HALO
    last = HALO + rows - 1
    loads = [
        pltpu.make_async_copy(src, dst, load_sem.at[3 + k])
        for k, (src, dst) in enumerate(small)
    ]

    def load_field(f):
        for y in range(rows):
            pltpu.make_async_copy(
                state.at[f, :, y, :], ext.at[f, first + y], load_sem.at[f]
            ).start()

    loads[0].start()
    load_field(PR)

    barrier = pltpu.get_barrier_semaphore()

    def greet(to):
        pl.semaphore_signal(barrier, inc=1, device_id=to, device_id_type=MESH)

    beside_x = (east, west)
    early = (lon == n_lon - 1, lon > 0)
    soon = (early[0], early[1] & (lon < n_lon - 1))
    count = [flag.astype(jnp.int32) for flag in has]
    n_beside = count[0] + count[1]
    n_early = early[0].astype(jnp.int32) + early[1].astype(jnp.int32)

    def every(there, sem):
        def tell(to):
            pl.semaphore_signal(sem, inc=1, device_id=to, device_id_type=MESH)

        tell((comp, lat, there))
        tell((other, lat, there))
        for ns in (0, 1):

            @pl.when(has[ns])
            def _(ns=ns):
                tell((comp, beside[ns], there))

    for d in (0, 1):

        @pl.when(jnp.logical_not(early[d]))
        def _(d=d):
            every(beside_x[d], barrier)

    for ns in (0, 1):

        @pl.when(has[ns])
        def _(ns=ns):
            greet((comp, beside[ns], lon))

    @pl.when(comp == 0)
    def _():
        greet((other, lat, lon))

    def enter(extra):
        pl.semaphore_wait(barrier, n_beside + n_early * (2 + n_beside) + extra)
        for d in (0, 1):

            @pl.when(early[d])
            def _(d=d):
                every(beside_x[d], told_sem.at[1 - d])

        if extra:
            pl.semaphore_signal(
                other_sem, inc=1, device_id=(other, lat, lon), device_id_type=MESH
            )

    load_field(U)
    load_field(V)
    for copy in loads[1:]:
        copy.start()

    def wait_field(f):
        own = ext.at[f, pl.ds(first, rows)]
        pltpu.make_async_copy(own, own, load_sem.at[f]).wait()

    for ns in (0, 1):

        @pl.when(jnp.logical_not(has[ns]))
        def _(ns=ns):
            row_in[ns] = jnp.zeros(row_in.shape[1:], jnp.float32)
            land_y[ns] = jnp.zeros((8, cols), jnp.int32)
            for side in (0, 1):
                corner_in[side, ns] = jnp.zeros((8, cols), jnp.float32)

    present = [flag.astype(jnp.float32) for flag in has]
    lane = lax.broadcasted_iota(jnp.int32, (levels, cols), 1)
    lane8 = lax.broadcasted_iota(jnp.int32, (8, cols), 1)
    j, block = lax.rem(lane, SPAN), lane // SPAN
    j8, block8 = lax.rem(lane8, SPAN), lane8 // SPAN
    west8 = block8 < plan.half
    half_lane = lane[: levels // 2]
    by_size = {
        levels: (j, block),
        levels // 2: (lax.rem(half_lane, SPAN), half_lane // SPAN),
        8: (j8, block8),
    }

    def is_own(size):
        jj, blk = by_size[size]
        return ((blk < plan.half) & (jj >= HALO)) | ((blk >= plan.half) & (jj < HALO))

    stack = lambda x: jnp.concatenate([x] * groups, axis=0)

    def coriolis(row):
        angle = (row.astype(jnp.float32) + 0.5) / (n_lat * rows) - 0.5
        return CORIOLIS * jnp.sin(math.pi * angle)

    base_row = lat * rows - HALO
    fcor = coriolis(
        lax.broadcasted_iota(jnp.int32, (rows + 2 * HALO, cols), 0) + base_row
    )
    local8 = lax.rem(block8, plan.half)
    strip_fcor = [stack(coriolis(SETS * local8 + r + base_row)) for r in range(SETS)]

    def roll(x, by):
        by = by % cols
        return pltpu.roll(x, by, 1) if by else x

    def remote(src, dst, sent, got, to):
        return pltpu.make_async_remote_copy(
            src_ref=src,
            dst_ref=dst,
            send_sem=send_sem.at[sent],
            recv_sem=recv_sem.at[got],
            device_id=to,
            device_id_type=MESH,
        )

    def side_copies(k, to):
        return [
            remote(
                side_out.at[k, pl.ds(start, size)],
                side_in.at[k, pl.ds(start, size)],
                0,
                0,
                (comp, lat, to),
            )
            for start, size in ((0, levels), (levels, levels // 2))
        ]

    sides = [side_copies(0, east), side_copies(1, west)]

    def corner_copy(ns, side):
        return remote(
            corner_out.at[ns, side],
            corner_in.at[side, 1 - ns],
            1 + ns,
            1 + (1 - ns),
            (comp, beside[ns], (east, west)[side]),
        )

    def row_copies(ns):
        its = 1 - ns
        to = (comp, beside[ns], lon)
        start = 0 if ns == 0 else rows - 8
        return [
            remote(row_out.at[ns], row_in.at[its], 1 + ns, 3 + its, to),
            remote(land_in.at[pl.ds(start, 8)], land_y.at[its], 1 + ns, 3 + its, to),
        ]

    across = [
        remote(state.at[:, 0], surf.at[k], 0, 5, (other, lat, there))
        for k, there in enumerate((lon, east, west))
    ]

    side_size = side_out.shape[1]
    row_size = row_out.shape[1] + 8

    def wait_for(sem, size):
        view = sizer.at[pl.ds(0, size)]
        pltpu.make_async_copy(view, view, sem).wait()

    @pl.when(comp == 1)
    def _():
        enter(1)
        for d in (0, 1):

            @pl.when(soon[d])
            def _(d=d):
                across[1 + d].start()

        across[0].start()

    def pack(row):
        result = None
        for y in range(rows):
            d = plan.dense[y]
            turned = roll(row(y), SPAN * d + HALO)
            where = (block if turned.shape[0] == levels else block8) == d
            result = turned if result is None else jnp.where(where, turned, result)
        return result

    def pack_field(f):
        packed = pack(lambda y: ext[f, first + y])
        dense[f] = packed
        return packed

    loads[0].wait()
    dry = comp == 1
    mask = jnp.where(dry, land_v[...].astype(jnp.float32), 1.0)
    spread = jnp.broadcast_to
    qm = pack(lambda y: spread(mask[y : y + 1], (8, cols)))
    low = j < HALO
    wait_field(PR)
    qp = pack_field(PR)
    wait_field(U)
    qu = pack_field(U)
    across_by = SPAN * plan.half
    u_east = jnp.where(j == 0, stack(roll(qm, -2)), qu)
    u_west = jnp.where(j == SPAN - 1, stack(roll(qm, 3)), qu)
    side_out[0, pl.ds(0, levels)] = jnp.where(low, qp, roll(u_east, HALO))
    side_out[1, pl.ds(0, levels)] = jnp.where(
        low, roll(u_west, across_by + HALO), roll(qp, across_by)
    )
    @pl.when(comp == 0)
    def _():
        enter(0)

    turn = {PR: 0, U: -2, V: 2}

    def send_corner(ns, d):
        @pl.when(has[ns])
        def _():
            corner_copy(ns, d).start()

    def corner(ns):
        its = 1 - ns
        picked = (0, 1) if ns == 0 else (rows - 2, rows - 1)
        found = {}
        for f in (U, V, PR):
            total = jnp.zeros((8, cols), jnp.float32)
            for k, y in enumerate(picked):
                value = ext[f, first + y]
                for g in range(groups):
                    b = (SLOTS[g] + plan.corner(0, its) + 2 * k) % plan.blocks
                    piece = roll(value[8 * g : 8 * g + 8], SPAN * b + HALO + turn[f])
                    total = jnp.where(block8 == b, piece, total)
            found[f] = total
        for f in (U, V, PR):
            row_out[ns, pl.ds(ROWS * levels + 8 * f, 8)] = found[f]
        to_east = jnp.where(j8 < 2, found[U], jnp.where(j8 < 4, found[PR], found[V]))
        to_west = jnp.where(j8 < 4, found[U], jnp.where(j8 < 6, found[PR], found[V]))
        corner_out[ns, 0] = to_east
        corner_out[ns, 1] = roll(to_west, across_by)
        for d in (0, 1):

            @pl.when(soon[d])
            def _(d=d):
                send_corner(ns, d)

    for d in (0, 1):

        @pl.when(soon[d])
        def _(d=d):
            sides[d][0].start()

    wait_field(V)

    @pl.when(has[0])
    def _():
        corner(0)

    qv = pack_field(V)
    mid_level = levels // 2
    half_low = low[:mid_level]
    v_east = jnp.where(j == 0, stack(roll(qm, -3)), qv)
    v_west = jnp.where(j == SPAN - 1, stack(roll(qm, 2)), qv)
    side_out[0, pl.ds(levels, mid_level)] = jnp.where(
        half_low, v_east[:mid_level], roll(v_east[mid_level:], HALO)
    )
    side_out[1, pl.ds(levels, mid_level)] = jnp.where(
        half_low,
        roll(v_west[mid_level:], across_by + HALO),
        roll(v_west[:mid_level], across_by),
    )

    for d in (0, 1):

        @pl.when(soon[d])
        def _(d=d):
            sides[d][1].start()

    @pl.when(has[1])
    def _():
        corner(1)

    for copy in loads[1:4]:
        copy.wait()

    diag = lax.broadcasted_iota(jnp.int32, (levels, levels), 0) == lax.broadcasted_iota(
        jnp.int32, (levels, levels), 1
    )

    def per_level(ref):
        wide = spread(ref[...], (levels, levels))
        column = jnp.sum(jnp.where(diag, wide, 0.0), axis=1, keepdims=True)
        return spread(column * 0.5, (levels, cols))

    hp = per_level(push_v)
    hf = per_level(fill_v)
    vert = vert_v[...]
    vert_hi = vert.astype(jnp.bfloat16).astype(jnp.float32)
    vert_cat = jnp.concatenate([vert_hi, vert_hi, vert - vert_hi], axis=1).astype(
        jnp.bfloat16
    )

    def split(x):
        hi = x.astype(jnp.bfloat16)
        lo = (x - hi.astype(jnp.float32)).astype(jnp.bfloat16)
        return jnp.concatenate([hi, lo, hi], axis=0)

    def product(pieces):
        result = jnp.dot(
            vert_cat,
            jnp.concatenate([split(x) for x in pieces], axis=1),
            preferred_element_type=jnp.float32,
        )
        return [result[:, i * cols : (i + 1) * cols] for i in range(len(pieces))]


    is_first, is_last = lane == 0, lane == cols - 1

    def span_x(x):
        return jnp.where(is_last, 0.0, roll(x, -1)) - jnp.where(is_first, 0.0, roll(x, 1))

    beyond_mask = []

    def keep(e):
        if e < first:
            return beyond_mask[0][e + 8 - first : e + 9 - first]
        if e > last:
            return beyond_mask[1][e - last - 1 : e - last]
        return mask[e - first : e - first + 1]

    def force(e):
        return fcor[e : e + 1]

    def advance_v(read, store, es):
        for e in es:
            v1 = read(V, e) - hp * (read(PR, e + 1) - read(PR, e - 1)) - force(e) * read(U, e)
            store[e] = v1

    def advance_u(read, e):
        u1 = read(U, e) + force(e) * read(V, e) - hp * span_x(read(PR, e))
        return u1, read(PR, e) - hf * span_x(u1)

    def add_v(store, e, value):
        return value - hf * (store[e + 1] - store[e - 1])

    def read_one(f, e):
        return ext[f, e]

    def read_two(f, e):
        return mid[f, e]

    def write_mid(f, e, value):
        mid[f, e] = keep(e) * value

    def write_main(f, e, value):
        main[f, e - first] = keep(e) * value

    def run(read, store, write, v_rows, u_rows, p_rows, v_kept, slot):
        advance_v(read, store, v_rows)
        for e in v_kept:
            write(V, e, store[e])
        ready = {}
        for e in u_rows:
            u1, partial = advance_u(read, e)
            write(U, e, u1)
            if e in p_rows:
                ready[e] = add_v(store, e, partial)
            else:
                part[slot[e]] = partial
        for e in p_rows:
            if e not in ready:
                ready[e] = add_v(store, e, part[slot[e]])
        for e, value in zip(p_rows, product([ready[e] for e in p_rows])):
            write(PR, e, value)

    slot_one = {first: 0, first + 1: 1, last - 1: 2, last: 3}
    slot_two = {first + 2: 4, first + 3: 5, last - 3: 6, last - 2: 7}
    span = lambda a, b: list(range(a, b + 1))

    toward = (1.0, -1.0)
    edges = ((first, first + 1, first + 2), (last, last - 1, last - 2))
    advance_v(read_one, vone, span(first + 1, first + 2) + span(last - 2, last - 1))
    for ns in (0, 1):
        a, b, c = edges[ns]
        sign = toward[ns]
        partial = {}
        for e in (a, b):
            u1, partial[e] = advance_u(read_one, e)
            mid[U, e] = keep(e) * u1
            part[slot_one[e]] = partial[e]
            if e == a:
                u_edge = u1
        w = ext[V, a] - sign * (hp * ext[PR, b]) - force(a) * ext[U, a]
        sent = (
            ext[PR, a],
            w,
            partial[a] - sign * (hf * vone[b]),
            partial[b] - sign * (hf * (vone[c] - w)),
            w - force(a) * u_edge,
        )
        for k, value in enumerate(sent):
            row_out[ns, pl.ds(k * levels, levels)] = value

    def send_rows():
        for even in (0, 1):
            for ns in (even, 1 - even):

                @pl.when(has[ns] & (lax.rem(lat, 2) == even))
                def _(ns=ns):
                    for copy in row_copies(ns):
                        copy.start()

    @pl.when(lon < n_lon - 1)
    def _():
        send_rows()

    run(
        read_one,
        vone,
        write_mid,
        span(first + 3, last - 3),
        span(first + 2, last - 2),
        span(first + 2, last - 2),
        span(first + 1, last - 1),
        slot_one,
    )
    @pl.when(lon == n_lon - 1)
    def _():
        send_rows()

    run(
        read_two,
        vtwo,
        write_main,
        span(first + 3, last - 3),
        span(first + 2, last - 2),
        span(first + 4, last - 4),
        span(first + 3, last - 3),
        slot_two,
    )

    for d in (0, 1):

        @pl.when(jnp.logical_not(early[d]))
        def _(d=d):
            pl.semaphore_wait(told_sem.at[d], 2 + n_beside)

        @pl.when(jnp.logical_not(soon[d]))
        def _(d=d):
            for copy in sides[d]:
                copy.start()
            for ns in (0, 1):
                send_corner(ns, d)

    for d in (0, 1):

        @pl.when(jnp.logical_not(soon[d]) | (comp == 0))
        def _(d=d):
            across[1 + d].start()

    @pl.when(comp == 0)
    def _():
        pl.semaphore_wait(other_sem, 1)
        across[0].start()

    for ns in (0, 1):

        @pl.when(has[ns])
        def _(ns=ns):
            wait_for(recv_sem.at[3 + ns], row_size)

    for ns in (0, 1):
        covered = jnp.where(dry, land_y[ns].astype(jnp.float32), 1.0)
        beyond_mask.append(present[ns] * covered)
    def got(ns, k):
        return row_in[ns, pl.ds(k * levels, levels)]

    ready = {}
    for ns in (0, 1):
        r, r2, r3 = edges[ns]
        a, b = (r - 1, r - 2) if ns == 0 else (r + 1, r + 2)
        sign = -toward[ns]
        p_r = ext[PR, r]
        v_r = ext[V, r] - sign * (hp * (got(ns, 0) - ext[PR, r2])) - force(r) * ext[U, r]
        v_a = present[ns] * (got(ns, 1) + sign * (hp * p_r))
        vone[r] = v_r
        mid[V, r] = keep(r) * v_r
        ready[r] = part[slot_one[r]] - sign * (hf * (v_a - vone[r2]))
        ready[r2] = part[slot_one[r2]] - sign * (hf * (v_r - vone[r3]))
        ready[a] = got(ns, 2) + sign * (hf * v_r)
        ready[b] = got(ns, 3) + hf * (hp * p_r)
    for e, value in zip(ready, product(list(ready.values()))):
        mid[PR, e] = keep(e) * value
    for ns in (0, 1):
        r = edges[ns][0]
        a, b = (r - 1, r - 2) if ns == 0 else (r + 1, r + 2)
        sign = -toward[ns]
        own_part = keep(a) * (got(ns, 4) + sign * (hp * ext[PR, r]))
        vtwo[a] = present[ns] * (own_part - sign * (hp * (mid[PR, b] - mid[PR, r])))
    run(
        read_two,
        vtwo,
        write_main,
        span(first, first + 2) + span(last - 2, last),
        [first, first + 1, last - 1, last],
        span(first, first + 3) + span(last - 3, last),
        span(first, first + 2) + span(last - 2, last),
        slot_two,
    )

    own = is_own(levels)

    def place(packed, rest, r, by, ours):
        jj, blk = by_size[packed.shape[0]]
        a, b = plan.span[r]
        in_west = (blk >= a) & (blk <= b)
        in_east = (blk >= plan.half + a) & (blk <= plan.half + b)
        lower = jj >= HALO if ours else jj < HALO
        upper = jj < HALO if ours else jj >= HALO
        flag = (in_west & lower) | (in_east & upper)
        return jnp.where(flag, roll(packed, SPAN * plan.shift[r] + by), rest)

    beyond_set = [plan.beyond[0][k] % SETS for k in (0, 1)]

    def place_beyond(below, above, k):
        b, t = k, plan.north + k
        size = below.shape[0]
        blk = by_size[size][1]
        both = jnp.where(blk == b, roll(below, SPAN * b + HALO), 0.0)
        both = jnp.where(blk == t, roll(above, SPAN * t + HALO), both)
        turned = roll(both, SPAN * plan.half)
        picked = jnp.where(blk < plan.half, both, turned)
        return jnp.where(is_own(size), picked, 0.0)

    zero = jnp.zeros((levels, cols), jnp.float32)
    zero8 = jnp.zeros((8, cols), jnp.float32)

    def slots_of(side, ns, k):
        return functools.reduce(
            jnp.logical_or,
            [
                block8 == (s + plan.corner(side, ns) + 2 * k) % plan.blocks
                for s in SLOTS[:groups]
            ],
        )

    def unfold(total, f, k):
        turned = [roll(total, -SPAN * (SLOTS[g] + k) - turn[f]) for g in range(groups)]
        return jnp.concatenate(turned, axis=0)

    def beyond_rows(f):
        rest = [zero] * SETS
        here = pl.ds(ROWS * levels + 8 * f, 8)
        for k in (0, 1):
            total = jnp.where(slots_of(0, 0, k), row_in[0, here], row_in[1, here])
            both = unfold(total, f, k)
            turned = roll(both, SPAN * plan.half)
            at = lax.rem(block, plan.half)
            picked = jnp.where(block < plan.half, both, turned)
            flag = ((at == k) | (at == plan.north + k)) & is_own(levels)
            rest[beyond_set[k]] = jnp.where(flag, picked, 0.0)
        return rest

    rest = [beyond_rows(f) for f in (U, V, PR)]
    rest_mask = [zero8] * SETS
    for k in (0, 1):
        rest_mask[beyond_set[k]] = place_beyond(
            spread(keep(plan.beyond[0][k]), (8, cols)),
            spread(keep(plan.beyond[1][k]), (8, cols)),
            k,
        )
    factor = [None] * SETS
    low_v, high_v = first - 1, last + 1
    for e, flag in ((low_v, present[0]), (high_v, present[1])):
        r = e % SETS
        at = local8 == e // SETS
        factor[r] = jnp.where(at, flag, 1.0 if factor[r] is None else factor[r])
    factor = [None if x is None else stack(x) for x in factor]

    def up(x):
        return [x[1], x[2], roll(x[0], -SPAN)]

    def down(x):
        return [roll(x[2], SPAN), x[0], x[1]]

    cut_low = (block >= plan.half) & (j == 0)
    cut_high = (block < plan.half) & (j == SPAN - 1)

    def strip_step(u, v, p, masks, only_own):
        def span_strip(x):
            ahead, back = roll(x, -1), roll(x, 1)
            change = jnp.where(cut_high, 0.0, ahead) - jnp.where(cut_low, 0.0, back)
            return jnp.where(own, change, 0.0) if only_own else change

        above, under = up(p), down(p)
        v1 = []
        for r in range(SETS):
            value = v[r] - hp * (above[r] - under[r]) - strip_fcor[r] * u[r]
            v1.append(value if factor[r] is None else factor[r] * value)
        u1 = [u[r] + strip_fcor[r] * v[r] - hp * span_strip(p[r]) for r in range(SETS)]
        above, under = up(v1), down(v1)
        p1 = [p[r] - hf * (span_strip(u1[r]) + above[r] - under[r]) for r in range(SETS)]
        p2 = product(p1)
        m = [stack(x) for x in masks]
        return (
            [m[r] * u1[r] for r in range(SETS)],
            [m[r] * v1[r] for r in range(SETS)],
            [m[r] * p2[r] for r in range(SETS)],
        )

    low8 = j8 < HALO
    for f in (U, V, PR):
        packed = dense[f]
        packed = jnp.where(low, roll(packed, across_by), packed)
        for r in range(SETS):
            strip[f, r] = place(packed, rest[f][r], r, 0, True)
    packed = jnp.where(low8, roll(qm, across_by), qm)
    own_masks = [place(packed, rest_mask[r], r, 0, True) for r in range(SETS)]
    strips = [[strip[f, r] for r in range(SETS)] for f in (U, V, PR)]
    for _ in range(2):
        strips = strip_step(*strips, own_masks, True)
    for f in (U, V, PR):
        for r in range(SETS):
            edge[f, r] = strips[f][r]

    for copy in loads[4:]:
        copy.wait()
    tiles = count_v[...].astype(jnp.float32)
    match = match_v[...]
    tile = lax.broadcasted_iota(jnp.int32, match.shape, 1)

    def coef(peer):
        mine = jnp.where((tile == lon) & (match == peer), tiles, 0.0)
        theirs = jnp.where((tile == peer) & (match == lon), tiles, 0.0)
        chosen = jnp.where(dry, mine, theirs)
        total = jnp.sum(jnp.sum(chosen, axis=1, keepdims=True), axis=0, keepdims=True)
        return spread(total, (rows, cols))

    coefs = [coef(lon), coef(west), coef(east)]
    inverse = KAPPA * mask / (coefs[0] + coefs[1] + coefs[2])
    scaled = [c * inverse for c in coefs]
    for f in (U, V, PR):
        top = ext[f, pl.ds(first, rows), 0, :]
        flux[f] = -KAPPA * mask * top

    wait_for(recv_sem.at[0], 2 * side_size)
    for ns in (0, 1):

        @pl.when(has[ns])
        def _(ns=ns):
            wait_for(recv_sem.at[1 + ns], 16)

    got_w, got_e = (side_in[k, pl.ds(0, levels)] for k in (0, 1))
    vw, ve = (side_in[k, pl.ds(levels, mid_level)] for k in (0, 1))
    corners = [[strip[f, r] for r in range(SETS)] for f in (U, V, PR)]
    for k in (0, 1):
        total = corner_in[0, 0]
        for side, ns in ((0, 1), (1, 0), (1, 1)):
            total = jnp.where(slots_of(side, ns, k), corner_in[side, ns], total)
        at = functools.reduce(
            jnp.logical_or,
            [
                (block == plan.corner(side, ns) + k) & (j // 2 == 1 + side)
                for side in (0, 1)
                for ns in (0, 1)
            ],
        )
        r = beyond_set[k]
        for f in (U, V, PR):
            corners[f][r] = jnp.where(at, unfold(total, f, k), corners[f][r])
    p_all = jnp.where(low, got_w, got_e)
    u_all = jnp.where(low, got_e, got_w)
    v_some = jnp.where(half_low, vw, ve)
    v_rest = jnp.where(half_low, ve, vw)
    strips = [
        [place(u_all, corners[U][r], r, -HALO, False) for r in range(SETS)],
        [
            jnp.concatenate(
                [
                    place(v_some, corners[V][r][:mid_level], r, 0, False),
                    place(v_rest, corners[V][r][mid_level:], r, -HALO, False),
                ],
                axis=0,
            )
            for r in range(SETS)
        ],
        [place(p_all, corners[PR][r], r, 0, False) for r in range(SETS)],
    ]
    mask_w = jnp.where(j8 == 2, roll(got_w[:8], -2), roll(vw[:8], 3))
    mask_e = jnp.where(j8 == HALO, roll(got_e[:8], -7), roll(ve[:8], -2))
    mask_all = jnp.where(low8, mask_w, mask_e)
    masks = [place(mask_all, own_masks[r], r, 0, False) for r in range(SETS)]
    strips = strip_step(*strips, masks, False)
    wait_for(recv_sem.at[5], 9 * rows)
    for f in (U, V, PR):
        value = flux[f]
        for k in range(3):
            value = value + scaled[k] * surf[k, f]
        flux[f] = value

    strips = strip_step(*strips, masks, False)
    for f in (U, V, PR):
        for r in range(SETS):
            change = strips[f][r] - edge[f, r]
            edge[f, r] = jnp.where(low, roll(change, across_by), change)

    wait_for(send_sem.at[0], 2 * side_size + 9 * rows)
    for ns in (0, 1):

        @pl.when(has[ns])
        def _(ns=ns):
            wait_for(send_sem.at[1 + ns], row_size + 16)


def finish(sizes, main, edge, flux, out, held, sem):
    levels, rows, cols = sizes
    plan = Layout(rows, cols)
    lane = lax.broadcasted_iota(jnp.int32, (levels, cols), 1)
    near = (lane < HALO) | (lane >= cols - HALO)
    top = lax.broadcasted_iota(jnp.int32, (8, cols), 0) == 0
    for y in range(rows):
        e = y + HALO
        by = -SPAN * (e // SETS) - HALO
        for f in (U, V, PR):
            change = pltpu.roll(edge[f, e % SETS], by % cols, 1)
            value = main[f, y] + jnp.where(near, change, 0.0)
            added = jnp.broadcast_to(flux[f, y : y + 1], (8, cols))
            held[f, y, 0:8] = value[0:8] + jnp.where(top, added, 0.0)
            held[f, y, 8:levels] = value[8:]
            pltpu.make_async_copy(held.at[f, y], out.at[f, :, y, :], sem.at[f]).start()
    for f in (U, V, PR):
        pltpu.make_async_copy(held.at[f], held.at[f], sem.at[f]).wait()


def shards(n_lat, n_lon, state, push, fill, vertical, land, match, counts):
    _, fields, levels, rows, cols = state.shape
    assert fields == 3 and levels % 16 == 0 and levels <= 32 and rows >= 16 and n_lon > 2
    f32 = jnp.float32
    any_spec = pl.BlockSpec(memory_space=pl.ANY)
    vmem_spec = pl.BlockSpec(memory_space=pltpu.VMEM)
    tall = rows + 2 * HALO
    line = (levels, cols)
    side_rows = levels + levels // 2
    main, edge, flux = pl.pallas_call(
        functools.partial(exchange, (levels, rows, cols, n_lat, n_lon)),
        out_shape=[
            pltpu.VMEM((fields, rows) + line, f32),
            pltpu.VMEM((fields, SETS) + line, f32),
            pltpu.VMEM((fields, rows, cols), f32),
        ],
        in_specs=[any_spec] * 7,
        out_specs=[vmem_spec] * 3,
        scratch_shapes=[
            pltpu.VMEM((fields, tall) + line, f32),
            pltpu.VMEM((fields, tall) + line, f32),
            pltpu.VMEM((tall,) + line, f32),
            pltpu.VMEM((tall,) + line, f32),
            pltpu.VMEM((8,) + line, f32),
            pltpu.VMEM((fields,) + line, f32),
            pltpu.VMEM((fields, SETS) + line, f32),
            pltpu.VMEM(push.shape, f32),
            pltpu.VMEM(fill.shape, f32),
            pltpu.VMEM(vertical.shape[1:], f32),
            pltpu.VMEM(land.shape, jnp.int32),
            pltpu.VMEM(match.shape[:0:-1], jnp.int32),
            pltpu.VMEM(counts.shape[:0:-1], jnp.int32),
            pltpu.VMEM((2, 8, cols), jnp.int32),
            pltpu.VMEM((2, side_rows, cols), f32),
            pltpu.VMEM((2, side_rows, cols), f32),
            pltpu.VMEM((2, ROWS * levels + 24, cols), f32),
            pltpu.VMEM((2, ROWS * levels + 24, cols), f32),
            pltpu.VMEM((2, 2, 8, cols), f32),
            pltpu.VMEM((2, 2, 8, cols), f32),
            pltpu.VMEM((3, fields, rows, cols), f32),
            pltpu.VMEM((ROWS * levels + 48 + 9 * rows, cols), f32),
            pltpu.SemaphoreType.DMA((9,)),
            pltpu.SemaphoreType.DMA((3,)),
            pltpu.SemaphoreType.DMA((6,)),
            pltpu.SemaphoreType.REGULAR((2,)),
            pltpu.SemaphoreType.REGULAR,
        ],
        compiler_params=pltpu.CompilerParams(collective_id=0, has_side_effects=True),
        name="exchange",
    )(
        state[0],
        push,
        fill,
        vertical.reshape(vertical.shape[1:]),
        land,
        match[0].T,
        counts[0].T,
    )
    main, edge, flux = (
        pltpu.with_memory_space_constraint(x, pltpu.VMEM) for x in (main, edge, flux)
    )
    result = pl.pallas_call(
        functools.partial(finish, (levels, rows, cols)),
        out_shape=jax.ShapeDtypeStruct(state.shape[1:], f32),
        in_specs=[vmem_spec] * 3,
        out_specs=any_spec,
        scratch_shapes=[
            pltpu.VMEM((fields, rows) + line, f32),
            pltpu.SemaphoreType.DMA((3,)),
        ],
        name="finish",
    )(main, edge, flux)
    return result[None]


def solution(mesh):
    sizes = dict(mesh.shape)
    return jax.shard_map(
        functools.partial(shards, sizes["lat"], sizes["lon"]),
        mesh=mesh,
        in_specs=(
            P("comp", None, None, "lat", "lon"),
            P("comp", None),
            P("comp", None),
            P("comp", None, None),
            P("lat", "lon"),
            P("lat", None, None),
            P("lat", None, None),
        ),
        out_specs=P("comp", None, None, "lat", "lon"),
        check_vma=False,
    )
```
